32 devices in a mesh: dp: 2 (over core), block: 16 (over z, y, x).
Axes of the slice: x: 2, y: 2, z: 4, core: 2. Of those that a mesh axis runs over, the one named last changes fastest.
Arguments:
- inputs: bfloat16 [8192, 2048], P('block', 'dp'), may hold values from -6 to 6
- grad_out: bfloat16 [8192, 2048], P('block', 'dp'), may hold values from -6 to 6
- right_first: bfloat16 [64, 128, 128], P('block'), may hold values from -0.5 to 0.5
- left_first: bfloat16 [128, 64, 64], P('block'), may hold values from -0.75 to 0.75
- right_gate: bfloat16 [64, 128, 128], P('block'), may hold values from -0.5 to 0.5
- left_gate: bfloat16 [128, 64, 64], P('block'), may hold values from -0.75 to 0.75
- right_mix: bfloat16 [64, 128, 128], P('block'), may hold values from -0.5 to 0.5
- left_mix: bfloat16 [128, 64, 64], P('block'), may hold values from -0.75 to 0.75
Outputs:
- outputs: bfloat16 [8192, 2048], P('block', 'dp')
- grad_in: bfloat16 [8192, 2048], P('block', 'dp')
- grad_right_first: float32 [64, 128, 128], P('block', 'dp')
- grad_left_first: float32 [128, 64, 64], P('block', 'dp')
- grad_right_gate: float32 [64, 128, 128], P('block', 'dp')
- grad_left_gate: float32 [128, 64, 64], P('block', 'dp')
- grad_right_mix: float32 [64, 128, 128], P('block', 'dp')
- grad_left_mix: float32 [128, 64, 64], P('block', 'dp')
The draws below stay inside these ranges and needn't reach their ends.
All inputs are finite; a program needn't handle non-finite values.
Results may differ from the reference program's by a relative error of at most 0.017.
Values may be sent and summed in bfloat16 or wider, within the bound.
A program may use at most 64 MiB of HBM per device.

```python
import jax
import jax.numpy as jnp
from jax import lax

NB = 64
BS = 128
TOK_DEV = 1024
D = 8192
TOKENS = 2048
N_DP = 2


def levels(key, extent, pieces, least, largest):
    level, own = 1.0, jax.random.fold_in(key, 6)
    for axis_at, shards_of in pieces:
        heights = jnp.exp(jax.random.uniform(jax.random.fold_in(own, axis_at), (shards_of,), jnp.float32, least / len(pieces), largest / len(pieces)))
        level = level * jnp.repeat(heights, extent[axis_at] // shards_of).reshape([-1 if axis == axis_at else 1 for axis in range(len(extent))])
    return level


def scatter_about(rng, dims, deviation, reach, shards=(), dtype=jnp.bfloat16):
    drawn = jax.random.normal(rng, dims, jnp.float32) * deviation
    if len(shards) > 0:
        drawn = levels(rng, dims, shards, -0.22, 0.18) * drawn
    return jnp.clip(drawn, min=-reach, max=reach).astype(dtype)


def setup_inputs(seed: int = 0) -> dict:
    arg_keys = jax.random.split(jax.random.key(seed), 9)
    inputs = scatter_about(arg_keys[0], (D, TOKENS), 1.0, 6.0, ((0, 16), (1, 2)))
    grad_out = scatter_about(arg_keys[1], (D, TOKENS), 1.0, 6.0, ((0, 16), (1, 2)))
    right_first = scatter_about(arg_keys[2], (NB, BS, BS), BS ** -0.5, 0.5, ((0, 16),))
    left_first = scatter_about(arg_keys[3], (BS, NB, NB), NB ** -0.5, 0.75, ((0, 16),))
    right_gate = scatter_about(arg_keys[4], (NB, BS, BS), BS ** -0.5, 0.5, ((0, 16),))
    left_gate = scatter_about(arg_keys[5], (BS, NB, NB), NB ** -0.5, 0.75, ((0, 16),))
    right_mix = scatter_about(arg_keys[6], (NB, BS, BS), BS ** -0.5, 0.5, ((0, 16),))
    left_mix = scatter_about(arg_keys[7], (BS, NB, NB), NB ** -0.5, 0.75, ((0, 16),))
    return dict(inputs=inputs, grad_out=grad_out, right_first=right_first, left_first=left_first, right_gate=right_gate, left_gate=left_gate, right_mix=right_mix, left_mix=left_mix)


def first_section(weight, values):
    nblocks = weight.shape[0]
    order = weight.shape[2]
    shaped = values.reshape(nblocks, order, -1).astype(jnp.float32)
    return jnp.einsum('bik,bkt->bit', weight.astype(jnp.float32), shaped).astype(jnp.bfloat16)


def second_section(weight, sectioned):
    mixed = jnp.einsum('jks,sjt->jkt', weight.astype(jnp.float32), sectioned.astype(jnp.float32))
    return mixed.reshape(-1, mixed.shape[2])


def backward_left(weight, sectioned, grad_rows):
    shaped = grad_rows.reshape(weight.shape[0], weight.shape[1], -1).astype(jnp.float32)
    grad_weight = jnp.einsum('jkt,sjt->jks', shaped, sectioned.astype(jnp.float32))
    back_rows = jnp.einsum('jks,jkt->sjt', weight.astype(jnp.float32), shaped).astype(jnp.bfloat16)
    return grad_weight, back_rows


def backward_right(weight, back_rows, values):
    shaped = values.reshape(weight.shape[0], weight.shape[2], -1).astype(jnp.float32)
    back_f = back_rows.astype(jnp.float32)
    grad_weight = jnp.einsum('bit,bkt->bik', back_f, shaped)
    grad_values = jnp.einsum('bik,bit->bkt', weight.astype(jnp.float32), back_f)
    return grad_weight, grad_values.reshape(-1, grad_values.shape[2])


def reference(inputs, grad_out, right_first, left_first, right_gate, left_gate, right_mix, left_mix):
    width = inputs.shape[0]
    sliced_in = inputs.reshape(width, N_DP, TOK_DEV).transpose(1, 0, 2)
    sliced_grad = grad_out.reshape(width, N_DP, TOK_DEV).transpose(1, 0, 2)

    def example(carry, pair):
        values, upstream = pair
        first_rows = first_section(right_first, values)
        gate_rows = first_section(right_gate, values)
        value = second_section(left_first, first_rows)
        gate = second_section(left_gate, gate_rows)
        sigma = jax.nn.sigmoid(gate)
        hidden = (value * gate * sigma).astype(jnp.bfloat16)
        mix_rows = first_section(right_mix, hidden)
        result = (values.astype(jnp.float32) + second_section(left_mix, mix_rows)).astype(jnp.bfloat16)
        g_left_mix, back_mix = backward_left(left_mix, mix_rows, upstream)
        g_right_mix, grad_hidden = backward_right(right_mix, back_mix, hidden)
        grad_value = (grad_hidden * gate * sigma).astype(jnp.bfloat16)
        grad_gate = (grad_hidden * value * sigma * (1.0 + gate * (1.0 - sigma))).astype(jnp.bfloat16)
        g_left_first, back_first = backward_left(left_first, first_rows, grad_value)
        g_left_gate, back_gate = backward_left(left_gate, gate_rows, grad_gate)
        g_right_first, through_first = backward_right(right_first, back_first, values)
        g_right_gate, through_gate = backward_right(right_gate, back_gate, values)
        grad_values = (upstream.astype(jnp.float32) + through_first + through_gate).astype(jnp.bfloat16)
        terms = (g_right_first, g_left_first, g_right_gate, g_left_gate, g_right_mix, g_left_mix)
        carry = tuple(c + t for c, t in zip(carry, terms))
        return carry, (result, grad_values)

    zeros_right = jnp.zeros(right_first.shape, jnp.float32)
    zeros_left = jnp.zeros(left_first.shape, jnp.float32)
    init = (zeros_right, zeros_left, zeros_right, zeros_left, zeros_right, zeros_left)
    grads, stacked = lax.scan(example, init, (sliced_in, sliced_grad))
    outputs = stacked[0].transpose(1, 0, 2).reshape(width, -1)
    grad_in = stacked[1].transpose(1, 0, 2).reshape(width, -1)
    return (outputs, grad_in, grads[0], grads[1], grads[2], grads[3], grads[4], grads[5])
```

```python
import functools

import jax
import jax.numpy as jnp
from jax import lax
from jax.experimental import pallas as pl
from jax.experimental.pallas import tpu as pltpu
from jax.sharding import PartitionSpec as P

F32 = jnp.float32
BF16 = jnp.bfloat16
CHUNKS = 2


def outgoing(weight, values, groups):
    shaped = values.reshape(weight.shape[0], weight.shape[2], -1)
    sectioned = jnp.einsum(
        "bik,bkt->bit", weight, shaped, preferred_element_type=jnp.float32
    ).astype(jnp.bfloat16)
    return sectioned.reshape(sectioned.shape[0], groups, -1, sectioned.shape[2])


def arrange(received):
    return received.reshape(-1, received.shape[2], received.shape[3])


def combine(weight, arranged):
    return jnp.einsum("jks,sjt->jkt", weight, arranged, preferred_element_type=jnp.float32)


def left_grads(weight, arranged, grad_rows, groups):
    grad_weight = jnp.einsum(
        "jkt,sjt->jks", grad_rows, arranged, preferred_element_type=jnp.float32
    )
    split_weight = weight.reshape(weight.shape[0], weight.shape[1], groups, -1)
    back_rows = jnp.einsum(
        "jkcr,jkt->rcjt", split_weight, grad_rows, preferred_element_type=jnp.float32
    )
    return (grad_weight, back_rows.astype(jnp.bfloat16))


def right_grads(weight, back_rows, values):
    shaped = values.reshape(weight.shape[0], weight.shape[2], -1)
    grad_weight = jnp.einsum("bit,bkt->bik", back_rows, shaped, preferred_element_type=jnp.float32)
    through = jnp.einsum("bik,bit->bkt", weight, back_rows, preferred_element_type=jnp.float32)
    return (grad_weight, through.reshape(-1, through.shape[2]))


def shards(inputs, grad_out, right_first, left_first, right_gate, left_gate, right_mix, left_mix):
    groups = lax.axis_size("block")
    rows, count = inputs.shape
    send_first = outgoing(right_first, inputs, groups)
    send_gate = outgoing(right_gate, inputs, groups)
    sectioned_first = arrange(
        lax.all_to_all(send_first, "block", split_axis=1, concat_axis=0, tiled=True)
    )
    sectioned_gate = arrange(
        lax.all_to_all(send_gate, "block", split_axis=1, concat_axis=0, tiled=True)
    )
    first_results = (
        combine(left_first, sectioned_first),
        combine(left_gate, sectioned_gate),
        sectioned_first,
        sectioned_gate,
    )
    value_parts = first_results[0]
    gate_parts = first_results[1]
    sectioned_first = first_results[2]
    sectioned_gate = first_results[3]
    value = value_parts.reshape(rows, count)
    gate = gate_parts.reshape(rows, count)
    sigma = jax.nn.sigmoid(gate)
    hidden = (value * gate * sigma).astype(jnp.bfloat16)
    send_mix = outgoing(right_mix, hidden, groups)
    sectioned = arrange(lax.all_to_all(send_mix, "block", split_axis=1, concat_axis=0, tiled=True))
    mixed_parts = combine(left_mix, sectioned)
    outputs = (inputs.astype(jnp.float32) + mixed_parts.reshape(rows, count)).astype(jnp.bfloat16)
    grad_rows = grad_out.reshape(left_mix.shape[0], left_mix.shape[1], count)
    grad_left_mix, back_mix = left_grads(left_mix, sectioned, grad_rows, groups)
    back_mix = lax.all_to_all(back_mix, "block", split_axis=1, concat_axis=1, tiled=True)
    back_mix = back_mix.reshape(right_mix.shape[0], right_mix.shape[1], count)
    grad_right_mix, grad_hidden = right_grads(right_mix, back_mix, hidden)
    grad_value = (grad_hidden * gate * sigma).astype(jnp.bfloat16)
    grad_gate = (grad_hidden * value * sigma * (1.0 + gate * (1.0 - sigma))).astype(jnp.bfloat16)
    value_rows = grad_value.reshape(left_first.shape[0], left_first.shape[1], count)
    gate_grad_rows = grad_gate.reshape(left_gate.shape[0], left_gate.shape[1], count)
    grad_left_first, back_first = left_grads(left_first, sectioned_first, value_rows, groups)
    grad_left_gate, back_gate = left_grads(left_gate, sectioned_gate, gate_grad_rows, groups)
    back_first, back_gate = (
        lax.all_to_all(back_first, "block", split_axis=1, concat_axis=1, tiled=True),
        lax.all_to_all(back_gate, "block", split_axis=1, concat_axis=1, tiled=True),
    )
    back_first = back_first.reshape(right_first.shape[0], right_first.shape[1], count)
    back_gate = back_gate.reshape(right_gate.shape[0], right_gate.shape[1], count)
    grad_right_first, through_first = right_grads(right_first, back_first, inputs)
    grad_right_gate, through_gate = right_grads(right_gate, back_gate, inputs)
    grad_in = (grad_out.astype(jnp.float32) + through_first + through_gate).astype(jnp.bfloat16)
    (
        summed_right_first,
        summed_left_first,
        summed_right_gate,
        summed_left_gate,
        summed_right_mix,
        summed_left_mix,
    ) = (
        lax.psum_scatter(
            grad_right_first.astype(jnp.bfloat16), "dp", scatter_dimension=1, tiled=True
        ).astype(jnp.float32),
        lax.psum_scatter(
            grad_left_first.astype(jnp.bfloat16), "dp", scatter_dimension=1, tiled=True
        ).astype(jnp.float32),
        lax.psum_scatter(
            grad_right_gate.astype(jnp.bfloat16), "dp", scatter_dimension=1, tiled=True
        ).astype(jnp.float32),
        lax.psum_scatter(
            grad_left_gate.astype(jnp.bfloat16), "dp", scatter_dimension=1, tiled=True
        ).astype(jnp.float32),
        lax.psum_scatter(
            grad_right_mix.astype(jnp.bfloat16), "dp", scatter_dimension=1, tiled=True
        ).astype(jnp.float32),
        lax.psum_scatter(
            grad_left_mix.astype(jnp.bfloat16), "dp", scatter_dimension=1, tiled=True
        ).astype(jnp.float32),
    )
    return (
        outputs,
        grad_in,
        summed_right_first,
        summed_left_first,
        summed_right_gate,
        summed_left_gate,
        summed_right_mix,
        summed_left_mix,
    )


def mm(a, b):
    return lax.dot_general(a, b, (((1,), (0,)), ((), ())), preferred_element_type=F32)


def mm_nt(a, b):
    return lax.dot_general(a, b, (((1,), (1,)), ((), ())), preferred_element_type=F32)


def fused_kernel(
    groups, nb, bs, jn, kn, chunks,
    in_ref, go_ref, rf_ref, lf_ref, rg_ref, lg_ref, rm_ref, lm_ref,
    out_ref, gin_ref, grf_ref, glf_ref, grg_ref, glg_ref, grm_ref, glm_ref,
    send_a, recv_a, send_b, recv_b, right_w, right_t, left_w, left_t, wide, gram_r, gram_l,
    right_send, right_recv, left_send, left_recv,
    send_sems, recv_sems, pair_send, pair_recv,
):
    me = lax.axis_index("block")
    dp = lax.axis_index("dp")
    other = 1 - dp
    rows, count = in_ref.shape
    tc = count // chunks
    piece = nb * jn

    barrier = pltpu.get_barrier_semaphore()

    @pl.loop(1, groups)
    def _(r):
        pl.semaphore_signal(barrier, inc=1, device_id={"block": lax.rem(me + r, groups)},
                            device_id_type=pl.DeviceIdType.MESH)

    pl.semaphore_signal(barrier, inc=1, device_id={"dp": other}, device_id_type=pl.DeviceIdType.MESH)

    def expand_right(m, ref):
        wide[...] = jnp.zeros_like(wide)
        for b in range(nb):
            wide[:, b, :, b * bs:(b + 1) * bs] = ref[b].astype(F32).reshape(groups, jn, bs)
        full = wide[...].reshape(rows, rows)
        right_w[m] = full.astype(BF16)
        right_t[m] = full.T.astype(BF16)

    spread = (
        lax.broadcasted_iota(jnp.int32, (rows, kn), 0) // jn
        == lax.broadcasted_iota(jnp.int32, (rows, kn), 1)
    ).astype(F32).astype(BF16)
    keep = (
        lax.broadcasted_iota(jnp.int32, (rows, rows), 0) // kn
        == lax.broadcasted_iota(jnp.int32, (rows, rows), 1) % jn
    )
    keep_t = (
        lax.broadcasted_iota(jnp.int32, (rows, rows), 0) % jn
        == lax.broadcasted_iota(jnp.int32, (rows, rows), 1) // kn
    )

    def expand_left(m, ref):
        flat = ref[...].reshape(rows, kn)
        left_w[m] = jnp.where(keep, mm_nt(flat, spread), 0.0).astype(BF16)
        left_t[m] = jnp.where(keep_t, mm_nt(spread, flat), 0.0).astype(BF16)

    def copy_to(phase, src, dst, c, r):
        peer = lax.rem(me + r, groups)
        return pltpu.make_async_remote_copy(
            src_ref=src.at[c, peer], dst_ref=dst.at[c, me],
            send_sem=send_sems.at[phase, c, r], recv_sem=recv_sems.at[phase, c, r],
            device_id={"block": peer}, device_id_type=pl.DeviceIdType.MESH,
        )

    def copy_from(phase, src, dst, c, r):
        peer = lax.rem(me + groups - r, groups)
        return pltpu.make_async_remote_copy(
            src_ref=src.at[c, peer], dst_ref=dst.at[c, peer],
            send_sem=send_sems.at[phase, c, r], recv_sem=recv_sems.at[phase, c, r],
            device_id={"block": peer}, device_id_type=pl.DeviceIdType.MESH,
        )

    def send(phase, src, dst, c):
        @pl.loop(1, groups)
        def _(r):
            copy_to(phase, src, dst, c, r).start()

        dst[c, me] = src[c, me]

    def receive(phase, src, dst, c):
        @pl.loop(1, groups)
        def _(r):
            copy_from(phase, src, dst, c, r).wait_recv()

    def columns(c):
        return pl.ds(pl.multiple_of(c * tc, tc), tc)

    def put(ref, c, m, result):
        ref[c, :, m] = result.astype(BF16).reshape(groups, piece, tc)

    def take(ref, c, m):
        return ref[c, :, m].reshape(rows, tc)

    expand_right(0, rf_ref)
    expand_right(1, rg_ref)
    expand_left(2, lm_ref)

    pl.semaphore_wait(barrier, groups)

    @pl.loop(0, chunks)
    def _(c):
        v = in_ref[:, columns(c)]
        put(send_a, c, 0, mm(right_w[0], v))
        put(send_a, c, 1, mm(right_w[1], v))
        put(send_a, c, 2, mm(left_t[2], go_ref[:, columns(c)]))
        send(0, send_a, recv_a, c)

    expand_right(2, rm_ref)
    expand_left(0, lf_ref)
    expand_left(1, lg_ref)
    gram_r[...] = jnp.zeros_like(gram_r)
    gram_l[...] = jnp.zeros_like(gram_l)

    @pl.loop(0, chunks)
    def _(c):
        receive(0, send_a, recv_a, c)
        first = take(recv_a, c, 0)
        gated = take(recv_a, c, 1)
        back = take(recv_a, c, 2)
        value = mm(left_w[0], first)
        gate = mm(left_w[1], gated)
        sigma = 1.0 / (1.0 + jnp.exp(-gate))
        silu = gate * sigma
        hidden = (value * silu).astype(BF16)
        put(send_b, c, 0, mm(right_w[2], hidden))
        grad_hidden = mm(right_t[2], back)
        grad_value = (grad_hidden * silu).astype(BF16)
        grad_gate = (grad_hidden * value * sigma * (1.0 + gate * (1.0 - sigma))).astype(BF16)
        put(send_b, c, 1, mm(left_t[0], grad_value))
        put(send_b, c, 2, mm(left_t[1], grad_gate))
        send(1, send_b, recv_b, c)
        gram_r[2] += mm_nt(back, hidden)
        gram_l[0] += mm_nt(grad_value, first)
        gram_l[1] += mm_nt(grad_gate, gated)

    half = bs // 2
    khalf = kn // 2

    def pick_right(m):
        full = gram_r[m].reshape(groups, nb, jn, rows)
        for b in range(nb):
            block = full[:, b, :, b * bs:(b + 1) * bs].reshape(2, half, bs)
            right_send[0, m, b] = block[0].astype(BF16)
            right_send[1, m, b] = block[1].astype(BF16)

    def pick_left(m):
        masked = jnp.where(keep, gram_l[m], 0.0).astype(BF16)
        picked = mm(masked, spread).reshape(jn, 2, khalf, kn)
        left_send[0, m] = picked[:, 0].astype(BF16)
        left_send[1, m] = picked[:, 1].astype(BF16)

    pick_right(2)
    pick_left(0)
    pick_left(1)

    @pl.loop(0, chunks)
    def _(c):
        receive(1, send_b, recv_b, c)
        mixed = take(recv_b, c, 0)
        back_first = take(recv_b, c, 1)
        back_gate = take(recv_b, c, 2)
        v = in_ref[:, columns(c)]
        g = go_ref[:, columns(c)]
        gram_l[2] += mm_nt(g, mixed)
        gram_r[0] += mm_nt(back_first, v)
        gram_r[1] += mm_nt(back_gate, v)
        out_ref[:, columns(c)] = (v.astype(F32) + mm(left_w[2], mixed)).astype(BF16)
        through = mm(right_t[0], back_first) + mm(right_t[1], back_gate)
        gin_ref[:, columns(c)] = (g.astype(F32) + through).astype(BF16)

    pick_left(2)
    pick_right(0)
    pick_right(1)

    pair = {"dp": other}
    swap_right = pltpu.make_async_remote_copy(
        src_ref=right_send.at[other], dst_ref=right_recv, send_sem=pair_send.at[0], recv_sem=pair_recv.at[0],
        device_id=pair, device_id_type=pl.DeviceIdType.MESH,
    )
    swap_left = pltpu.make_async_remote_copy(
        src_ref=left_send.at[other], dst_ref=left_recv, send_sem=pair_send.at[1], recv_sem=pair_recv.at[1],
        device_id=pair, device_id_type=pl.DeviceIdType.MESH,
    )
    swap_right.start()
    swap_left.start()

    @pl.loop(0, chunks)
    def _(c):
        @pl.loop(1, groups)
        def _(r):
            copy_to(0, send_a, recv_a, c, r).wait_send()
            copy_to(1, send_b, recv_b, c, r).wait_send()

    swap_right.wait()
    swap_left.wait()
    for m, ref in enumerate((grf_ref, grg_ref, grm_ref)):
        ref[...] = right_send[dp, m].astype(F32) + right_recv[m].astype(F32)
    for m, ref in enumerate((glf_ref, glg_ref, glm_ref)):
        ref[...] = left_send[dp, m].astype(F32) + left_recv[m].astype(F32)


def fused(inputs, grad_out, right_first, left_first, right_gate, left_gate, right_mix, left_mix):
    groups = lax.axis_size("block")
    rows, count = inputs.shape
    nb, bs, _ = right_first.shape
    jn, kn, _ = left_first.shape
    chunks = CHUNKS
    tc = count // chunks
    piece = nb * jn
    right_out = jax.ShapeDtypeStruct((nb, bs // 2, bs), F32)
    left_out = jax.ShapeDtypeStruct((jn, kn // 2, kn), F32)
    vmem = pl.BlockSpec(memory_space=pltpu.VMEM)
    moving = pltpu.VMEM((chunks, groups, 3, piece, tc), BF16)
    factor = pltpu.VMEM((3, rows, rows), BF16)
    return pl.pallas_call(
        functools.partial(fused_kernel, groups, nb, bs, jn, kn, chunks),
        out_shape=(
            jax.ShapeDtypeStruct(inputs.shape, BF16), jax.ShapeDtypeStruct(inputs.shape, BF16),
            right_out, left_out, right_out, left_out, right_out, left_out,
        ),
        in_specs=[vmem] * 8,
        out_specs=(vmem,) * 8,
        scratch_shapes=[
            moving, moving, moving, moving, factor, factor, factor, factor,
            pltpu.VMEM((groups, nb, jn, rows), F32),
            pltpu.VMEM((3, rows, rows), F32),
            pltpu.VMEM((3, rows, rows), F32),
            pltpu.VMEM((2, 3, nb, bs // 2, bs), BF16),
            pltpu.VMEM((3, nb, bs // 2, bs), BF16),
            pltpu.VMEM((2, 3, jn, kn // 2, kn), BF16),
            pltpu.VMEM((3, jn, kn // 2, kn), BF16),
            pltpu.SemaphoreType.DMA((2, chunks, groups)),
            pltpu.SemaphoreType.DMA((2, chunks, groups)),
            pltpu.SemaphoreType.DMA((2,)),
            pltpu.SemaphoreType.DMA((2,)),
        ],
        compiler_params=pltpu.CompilerParams(
            collective_id=0, has_side_effects=True, vmem_limit_bytes=60 * 1024 * 1024
        ),
    )(inputs, grad_out, right_first, left_first, right_gate, left_gate, right_mix, left_mix)


def layer(*args):
    groups, pairs = lax.axis_size("block"), lax.axis_size("dp")
    inputs, right, left = args[0], args[2], args[3]
    piece = right.shape[0] * left.shape[0]
    fits = (
        pairs == 2 and piece % 16 == 0 and left.shape[0] % 8 == 0 and right.shape[1] % 128 == 0
        and inputs.shape[1] % (128 * CHUNKS) == 0 and groups * piece == inputs.shape[0]
    )
    return fused(*args) if fits else shards(*args)


def solution(mesh):
    return jax.shard_map(
        layer,
        mesh=mesh,
        in_specs=(
            P("block", "dp"),
            P("block", "dp"),
            P("block", None, None),
            P("block", None, None),
            P("block", None, None),
            P("block", None, None),
            P("block", None, None),
            P("block", None, None),
        ),
        out_specs=(
            P("block", "dp"),
            P("block", "dp"),
            P("block", "dp", None),
            P("block", "dp", None),
            P("block", "dp", None),
            P("block", "dp", None),
            P("block", "dp", None),
            P("block", "dp", None),
        ),
        check_vma=False,
    )
```

```python
import functools

import jax
import jax.numpy as jnp
from jax import lax
from jax.experimental import pallas as pl
from jax.experimental.pallas import tpu as pltpu
from jax.sharding import PartitionSpec as P

F32 = jnp.float32
BF16 = jnp.bfloat16
CHUNKS = 4


def outgoing(weight, values, groups):
    shaped = values.reshape(weight.shape[0], weight.shape[2], -1)
    sectioned = jnp.einsum(
        "bik,bkt->bit", weight, shaped, preferred_element_type=jnp.float32
    ).astype(jnp.bfloat16)
    return sectioned.reshape(sectioned.shape[0], groups, -1, sectioned.shape[2])


def arrange(received):
    return received.reshape(-1, received.shape[2], received.shape[3])


def combine(weight, arranged):
    return jnp.einsum("jks,sjt->jkt", weight, arranged, preferred_element_type=jnp.float32)


def left_grads(weight, arranged, grad_rows, groups):
    grad_weight = jnp.einsum(
        "jkt,sjt->jks", grad_rows, arranged, preferred_element_type=jnp.float32
    )
    split_weight = weight.reshape(weight.shape[0], weight.shape[1], groups, -1)
    back_rows = jnp.einsum(
        "jkcr,jkt->rcjt", split_weight, grad_rows, preferred_element_type=jnp.float32
    )
    return (grad_weight, back_rows.astype(jnp.bfloat16))


def right_grads(weight, back_rows, values):
    shaped = values.reshape(weight.shape[0], weight.shape[2], -1)
    grad_weight = jnp.einsum("bit,bkt->bik", back_rows, shaped, preferred_element_type=jnp.float32)
    through = jnp.einsum("bik,bit->bkt", weight, back_rows, preferred_element_type=jnp.float32)
    return (grad_weight, through.reshape(-1, through.shape[2]))


def shards(inputs, grad_out, right_first, left_first, right_gate, left_gate, right_mix, left_mix):
    groups = lax.axis_size("block")
    rows, count = inputs.shape
    send_first = outgoing(right_first, inputs, groups)
    send_gate = outgoing(right_gate, inputs, groups)
    sectioned_first = arrange(
        lax.all_to_all(send_first, "block", split_axis=1, concat_axis=0, tiled=True)
    )
    sectioned_gate = arrange(
        lax.all_to_all(send_gate, "block", split_axis=1, concat_axis=0, tiled=True)
    )
    first_results = (
        combine(left_first, sectioned_first),
        combine(left_gate, sectioned_gate),
        sectioned_first,
        sectioned_gate,
    )
    value_parts = first_results[0]
    gate_parts = first_results[1]
    sectioned_first = first_results[2]
    sectioned_gate = first_results[3]
    value = value_parts.reshape(rows, count)
    gate = gate_parts.reshape(rows, count)
    sigma = jax.nn.sigmoid(gate)
    hidden = (value * gate * sigma).astype(jnp.bfloat16)
    send_mix = outgoing(right_mix, hidden, groups)
    sectioned = arrange(lax.all_to_all(send_mix, "block", split_axis=1, concat_axis=0, tiled=True))
    mixed_parts = combine(left_mix, sectioned)
    outputs = (inputs.astype(jnp.float32) + mixed_parts.reshape(rows, count)).astype(jnp.bfloat16)
    grad_rows = grad_out.reshape(left_mix.shape[0], left_mix.shape[1], count)
    grad_left_mix, back_mix = left_grads(left_mix, sectioned, grad_rows, groups)
    back_mix = lax.all_to_all(back_mix, "block", split_axis=1, concat_axis=1, tiled=True)
    back_mix = back_mix.reshape(right_mix.shape[0], right_mix.shape[1], count)
    grad_right_mix, grad_hidden = right_grads(right_mix, back_mix, hidden)
    grad_value = (grad_hidden * gate * sigma).astype(jnp.bfloat16)
    grad_gate = (grad_hidden * value * sigma * (1.0 + gate * (1.0 - sigma))).astype(jnp.bfloat16)
    value_rows = grad_value.reshape(left_first.shape[0], left_first.shape[1], count)
    gate_grad_rows = grad_gate.reshape(left_gate.shape[0], left_gate.shape[1], count)
    grad_left_first, back_first = left_grads(left_first, sectioned_first, value_rows, groups)
    grad_left_gate, back_gate = left_grads(left_gate, sectioned_gate, gate_grad_rows, groups)
    back_first, back_gate = (
        lax.all_to_all(back_first, "block", split_axis=1, concat_axis=1, tiled=True),
        lax.all_to_all(back_gate, "block", split_axis=1, concat_axis=1, tiled=True),
    )
    back_first = back_first.reshape(right_first.shape[0], right_first.shape[1], count)
    back_gate = back_gate.reshape(right_gate.shape[0], right_gate.shape[1], count)
    grad_right_first, through_first = right_grads(right_first, back_first, inputs)
    grad_right_gate, through_gate = right_grads(right_gate, back_gate, inputs)
    grad_in = (grad_out.astype(jnp.float32) + through_first + through_gate).astype(jnp.bfloat16)
    (
        summed_right_first,
        summed_left_first,
        summed_right_gate,
        summed_left_gate,
        summed_right_mix,
        summed_left_mix,
    ) = (
        lax.psum_scatter(
            grad_right_first.astype(jnp.bfloat16), "dp", scatter_dimension=1, tiled=True
        ).astype(jnp.float32),
        lax.psum_scatter(
            grad_left_first.astype(jnp.bfloat16), "dp", scatter_dimension=1, tiled=True
        ).astype(jnp.float32),
        lax.psum_scatter(
            grad_right_gate.astype(jnp.bfloat16), "dp", scatter_dimension=1, tiled=True
        ).astype(jnp.float32),
        lax.psum_scatter(
            grad_left_gate.astype(jnp.bfloat16), "dp", scatter_dimension=1, tiled=True
        ).astype(jnp.float32),
        lax.psum_scatter(
            grad_right_mix.astype(jnp.bfloat16), "dp", scatter_dimension=1, tiled=True
        ).astype(jnp.float32),
        lax.psum_scatter(
            grad_left_mix.astype(jnp.bfloat16), "dp", scatter_dimension=1, tiled=True
        ).astype(jnp.float32),
    )
    return (
        outputs,
        grad_in,
        summed_right_first,
        summed_left_first,
        summed_right_gate,
        summed_left_gate,
        summed_right_mix,
        summed_left_mix,
    )


def mm(a, b):
    return lax.dot_general(a, b, (((1,), (0,)), ((), ())), preferred_element_type=F32)


def mm_nt(a, b):
    return lax.dot_general(a, b, (((1,), (1,)), ((), ())), preferred_element_type=F32)


def fused_kernel(
    groups, nb, bs, jn, kn, chunks,
    in_ref, go_ref, rf_ref, lf_ref, rg_ref, lg_ref, rm_ref, lm_ref,
    out_ref, gin_ref, gr_ref, gl_ref,
    send_a, recv_a, send_b, recv_b, right_w, right_t, left_w, left_t, wide, gram_r, gram_l,
    right_send, right_recv, left_send, left_recv,
    send_sems, recv_sems, pair_send, pair_recv,
):
    me = lax.axis_index("block")
    dp = lax.axis_index("dp")
    other = 1 - dp
    rows, count = in_ref.shape
    tc = count // chunks
    piece = nb * jn

    barrier = pltpu.get_barrier_semaphore()

    @pl.loop(1, groups)
    def _(r):
        pl.semaphore_signal(barrier, inc=1, device_id={"block": lax.rem(me + r, groups)},
                            device_id_type=pl.DeviceIdType.MESH)

    pl.semaphore_signal(barrier, inc=1, device_id={"dp": other}, device_id_type=pl.DeviceIdType.MESH)

    def expand_right(m, ref):
        wide[...] = jnp.zeros_like(wide)
        for b in range(nb):
            wide[:, b, :, b * bs:(b + 1) * bs] = ref[b].astype(F32).reshape(groups, jn, bs)
        full = wide[...].reshape(rows, rows)
        right_w[m] = full.astype(BF16)

    def turn_right(m):
        right_t[m] = right_w[m].astype(F32).T.astype(BF16)

    spread = (
        lax.broadcasted_iota(jnp.int32, (rows, kn), 0) // jn
        == lax.broadcasted_iota(jnp.int32, (rows, kn), 1)
    ).astype(F32).astype(BF16)
    keep = (
        lax.broadcasted_iota(jnp.int32, (rows, rows), 0) // kn
        == lax.broadcasted_iota(jnp.int32, (rows, rows), 1) % jn
    )
    keep_t = (
        lax.broadcasted_iota(jnp.int32, (rows, rows), 0) % jn
        == lax.broadcasted_iota(jnp.int32, (rows, rows), 1) // kn
    )

    def expand_left(m, ref):
        left_w[m] = jnp.where(keep, mm_nt(ref[...].reshape(rows, kn), spread), 0.0).astype(BF16)

    def turn_left(m, ref):
        left_t[m] = jnp.where(keep_t, mm_nt(spread, ref[...].reshape(rows, kn)), 0.0).astype(BF16)

    def copy_to(phase, src, dst, c, r):
        peer = lax.rem(me + r, groups)
        return pltpu.make_async_remote_copy(
            src_ref=src.at[c, peer], dst_ref=dst.at[c, me],
            send_sem=send_sems.at[phase, c, r], recv_sem=recv_sems.at[phase, c, r],
            device_id={"block": peer}, device_id_type=pl.DeviceIdType.MESH,
        )

    def copy_from(phase, src, dst, c, r):
        peer = lax.rem(me + groups - r, groups)
        return pltpu.make_async_remote_copy(
            src_ref=src.at[c, peer], dst_ref=dst.at[c, peer],
            send_sem=send_sems.at[phase, c, r], recv_sem=recv_sems.at[phase, c, r],
            device_id={"block": peer}, device_id_type=pl.DeviceIdType.MESH,
        )

    def send(phase, src, dst, c):
        @pl.loop(0, groups - 1)
        def _(n):
            r = groups // 2 + (1 - 2 * lax.rem(n, 2)) * ((n + 1) // 2)
            copy_to(phase, src, dst, c, r).start()

        dst[c, me] = src[c, me]

    def receive(phase, src, dst, c):
        @pl.loop(1, groups)
        def _(r):
            copy_from(phase, src, dst, c, r).wait_recv()

    def columns(c):
        return pl.ds(pl.multiple_of(c * tc, tc), tc)

    def put(ref, c, m, result):
        ref[c, :, m] = result.astype(BF16).reshape(groups, piece, tc)

    def take(ref, c, m):
        return ref[c, :, m].reshape(rows, tc)

    expand_right(0, rf_ref)
    expand_right(1, rg_ref)
    turn_left(2, lm_ref)

    pl.semaphore_wait(barrier, groups)

    @pl.loop(0, chunks)
    def _(c):
        v = in_ref[:, columns(c)]
        put(send_a, c, 0, mm(right_w[0], v))
        put(send_a, c, 1, mm(right_w[1], v))
        put(send_a, c, 2, mm(left_t[2], go_ref[:, columns(c)]))
        send(0, send_a, recv_a, c)

    expand_left(0, lf_ref)
    expand_left(1, lg_ref)
    expand_right(2, rm_ref)
    turn_right(2)
    turn_left(0, lf_ref)
    turn_left(1, lg_ref)
    gram_r[...] = jnp.zeros_like(gram_r)
    gram_l[...] = jnp.zeros_like(gram_l)

    @pl.loop(0, chunks)
    def _(c):
        receive(0, send_a, recv_a, c)
        first = take(recv_a, c, 0)
        gated = take(recv_a, c, 1)
        back = take(recv_a, c, 2)
        value = mm(left_w[0], first)
        gate = mm(left_w[1], gated)
        sigma = 1.0 / (1.0 + jnp.exp(-gate))
        silu = gate * sigma
        hidden = (value * silu).astype(BF16)
        put(send_b, c, 0, mm(right_w[2], hidden))
        grad_hidden = mm(right_t[2], back)
        grad_value = (grad_hidden * silu).astype(BF16)
        grad_gate = (grad_hidden * value * sigma * (1.0 + gate * (1.0 - sigma))).astype(BF16)
        put(send_b, c, 1, mm(left_t[0], grad_value))
        put(send_b, c, 2, mm(left_t[1], grad_gate))
        send(1, send_b, recv_b, c)
        gram_r[2] += mm_nt(back, hidden)
        gram_l[0] += mm_nt(grad_value, first)
        gram_l[1] += mm_nt(grad_gate, gated)

    half = bs // 2
    khalf = kn // 2

    def pick_right(m):
        full = gram_r[m].reshape(groups, nb, jn, rows)
        for b in range(nb):
            block = full[:, b, :, b * bs:(b + 1) * bs].reshape(2, half, bs)
            right_send[0, m, b] = block[0].astype(BF16)
            right_send[1, m, b] = block[1].astype(BF16)

    def pick_left(m):
        masked = jnp.where(keep, gram_l[m], 0.0).astype(BF16)
        picked = mm(masked, spread).reshape(jn, 2, khalf, kn)
        left_send[0, m] = picked[:, 0].astype(BF16)
        left_send[1, m] = picked[:, 1].astype(BF16)

    pair = {"dp": other}

    def swap(n, src, dst):
        return pltpu.make_async_remote_copy(
            src_ref=src, dst_ref=dst, send_sem=pair_send.at[n], recv_sem=pair_recv.at[n],
            device_id=pair, device_id_type=pl.DeviceIdType.MESH,
        )

    swaps = [
        swap(0, right_send.at[other, 2], right_recv.at[2]),
        swap(1, left_send.at[other, pl.ds(0, 2)], left_recv.at[pl.ds(0, 2)]),
        swap(2, right_send.at[other, pl.ds(0, 2)], right_recv.at[pl.ds(0, 2)]),
        swap(3, left_send.at[other, 2], left_recv.at[2]),
    ]
    pick_right(2)
    pick_left(0)
    pick_left(1)
    swaps[0].start()
    swaps[1].start()
    turn_right(0)
    turn_right(1)
    expand_left(2, lm_ref)

    def last_grams(c):
        receive(1, send_b, recv_b, c)
        gram_l[2] += mm_nt(go_ref[:, columns(c)], take(recv_b, c, 0))
        v = in_ref[:, columns(c)]
        gram_r[0] += mm_nt(take(recv_b, c, 1), v)
        gram_r[1] += mm_nt(take(recv_b, c, 2), v)

    def last_rows(c):
        v = in_ref[:, columns(c)]
        g = go_ref[:, columns(c)]
        out_ref[:, columns(c)] = (v.astype(F32) + mm(left_w[2], take(recv_b, c, 0))).astype(BF16)
        through = mm(right_t[0], take(recv_b, c, 1)) + mm(right_t[1], take(recv_b, c, 2))
        gin_ref[:, columns(c)] = (g.astype(F32) + through).astype(BF16)

    @pl.loop(0, chunks - 1)
    def _(c):
        last_grams(c)
        last_rows(c)

    last_grams(chunks - 1)
    pick_left(2)
    pick_right(0)
    pick_right(1)
    swaps[2].start()
    swaps[3].start()
    last_rows(chunks - 1)

    @pl.loop(0, chunks)
    def _(c):
        @pl.loop(1, groups)
        def _(r):
            copy_to(0, send_a, recv_a, c, r).wait_send()
            copy_to(1, send_b, recv_b, c, r).wait_send()

    for each in swaps:
        each.wait()
    gr_ref[...] = right_send[dp].astype(F32) + right_recv[...].astype(F32)
    gl_ref[...] = left_send[dp].astype(F32) + left_recv[...].astype(F32)


def results_kernel(out_in, gin_in, gr_in, gl_in, out, gin, grf, glf, grg, glg, grm, glm, sems):
    moves = [(out_in, out), (gin_in, gin)]
    moves += [(gr_in.at[m], ref) for m, ref in enumerate((grf, grg, grm))]
    moves += [(gl_in.at[m], ref) for m, ref in enumerate((glf, glg, glm))]
    copies = [pltpu.make_async_copy(src, dst, sems.at[n]) for n, (src, dst) in enumerate(moves)]
    for copy in copies:
        copy.start()
    for copy in copies:
        copy.wait()


def fused(inputs, grad_out, right_first, left_first, right_gate, left_gate, right_mix, left_mix):
    groups = lax.axis_size("block")
    rows, count = inputs.shape
    nb, bs, _ = right_first.shape
    jn, kn, _ = left_first.shape
    chunks = CHUNKS
    tc = count // chunks
    piece = nb * jn
    right_out = jax.ShapeDtypeStruct((nb, bs // 2, bs), F32)
    left_out = jax.ShapeDtypeStruct((jn, kn // 2, kn), F32)
    vmem = pl.BlockSpec(memory_space=pltpu.VMEM)
    moving = pltpu.VMEM((chunks, groups, 3, piece, tc), BF16)
    factor = pltpu.VMEM((3, rows, rows), BF16)
    moved = pl.pallas_call(
        functools.partial(fused_kernel, groups, nb, bs, jn, kn, chunks),
        out_shape=(
            jax.ShapeDtypeStruct(inputs.shape, BF16), jax.ShapeDtypeStruct(inputs.shape, BF16),
            jax.ShapeDtypeStruct((3,) + right_out.shape, F32), jax.ShapeDtypeStruct((3,) + left_out.shape, F32),
        ),
        in_specs=[vmem] * 8,
        out_specs=(vmem,) * 4,
        scratch_shapes=[
            moving, moving, moving, moving, factor, factor, factor, factor,
            pltpu.VMEM((groups, nb, jn, rows), F32),
            pltpu.VMEM((3, rows, rows), F32),
            pltpu.VMEM((3, rows, rows), F32),
            pltpu.VMEM((2, 3, nb, bs // 2, bs), BF16),
            pltpu.VMEM((3, nb, bs // 2, bs), BF16),
            pltpu.VMEM((2, 3, jn, kn // 2, kn), BF16),
            pltpu.VMEM((3, jn, kn // 2, kn), BF16),
            pltpu.SemaphoreType.DMA((2, chunks, groups)),
            pltpu.SemaphoreType.DMA((2, chunks, groups)),
            pltpu.SemaphoreType.DMA((4,)),
            pltpu.SemaphoreType.DMA((4,)),
        ],
        compiler_params=pltpu.CompilerParams(
            collective_id=0, has_side_effects=True, vmem_limit_bytes=60 * 1024 * 1024
        ),
    )(inputs, grad_out, right_first, left_first, right_gate, left_gate, right_mix, left_mix)
    anywhere = pl.BlockSpec(memory_space=pl.ANY)
    return pl.pallas_call(
        results_kernel,
        out_shape=(
            jax.ShapeDtypeStruct(inputs.shape, BF16), jax.ShapeDtypeStruct(inputs.shape, BF16),
            right_out, left_out, right_out, left_out, right_out, left_out,
        ),
        in_specs=[anywhere] * 4,
        out_specs=(anywhere,) * 8,
        scratch_shapes=[pltpu.SemaphoreType.DMA((8,))],
    )(*moved)


def layer(*args):
    groups, pairs = lax.axis_size("block"), lax.axis_size("dp")
    inputs, right, left = args[0], args[2], args[3]
    piece = right.shape[0] * left.shape[0]
    fits = (
        pairs == 2 and piece % 16 == 0 and left.shape[0] % 8 == 0 and right.shape[1] % 128 == 0
        and inputs.shape[1] % (128 * CHUNKS) == 0 and groups * piece == inputs.shape[0]
    )
    return fused(*args) if fits else shards(*args)


def solution(mesh):
    return jax.shard_map(
        layer,
        mesh=mesh,
        in_specs=(
            P("block", "dp"),
            P("block", "dp"),
            P("block", None, None),
            P("block", None, None),
            P("block", None, None),
            P("block", None, None),
            P("block", None, None),
            P("block", None, None),
        ),
        out_specs=(
            P("block", "dp"),
            P("block", "dp"),
            P("block", "dp", None),
            P("block", "dp", None),
            P("block", "dp", None),
            P("block", "dp", None),
            P("block", "dp", None),
            P("block", "dp", None),
        ),
        check_vma=False,
    )
```

```python
import functools

import jax
import jax.numpy as jnp
from jax import lax
from jax.experimental import pallas as pl
from jax.experimental.pallas import tpu as pltpu
from jax.sharding import PartitionSpec as P

F32 = jnp.float32
BF16 = jnp.bfloat16
CHUNKS = 4


def outgoing(weight, values, groups):
    shaped = values.reshape(weight.shape[0], weight.shape[2], -1)
    sectioned = jnp.einsum(
        "bik,bkt->bit", weight, shaped, preferred_element_type=jnp.float32
    ).astype(jnp.bfloat16)
    return sectioned.reshape(sectioned.shape[0], groups, -1, sectioned.shape[2])


def arrange(received):
    return received.reshape(-1, received.shape[2], received.shape[3])


def combine(weight, arranged):
    return jnp.einsum("jks,sjt->jkt", weight, arranged, preferred_element_type=jnp.float32)


def left_grads(weight, arranged, grad_rows, groups):
    grad_weight = jnp.einsum(
        "jkt,sjt->jks", grad_rows, arranged, preferred_element_type=jnp.float32
    )
    split_weight = weight.reshape(weight.shape[0], weight.shape[1], groups, -1)
    back_rows = jnp.einsum(
        "jkcr,jkt->rcjt", split_weight, grad_rows, preferred_element_type=jnp.float32
    )
    return (grad_weight, back_rows.astype(jnp.bfloat16))


def right_grads(weight, back_rows, values):
    shaped = values.reshape(weight.shape[0], weight.shape[2], -1)
    grad_weight = jnp.einsum("bit,bkt->bik", back_rows, shaped, preferred_element_type=jnp.float32)
    through = jnp.einsum("bik,bit->bkt", weight, back_rows, preferred_element_type=jnp.float32)
    return (grad_weight, through.reshape(-1, through.shape[2]))


def shards(inputs, grad_out, right_first, left_first, right_gate, left_gate, right_mix, left_mix):
    groups = lax.axis_size("block")
    rows, count = inputs.shape
    send_first = outgoing(right_first, inputs, groups)
    send_gate = outgoing(right_gate, inputs, groups)
    sectioned_first = arrange(
        lax.all_to_all(send_first, "block", split_axis=1, concat_axis=0, tiled=True)
    )
    sectioned_gate = arrange(
        lax.all_to_all(send_gate, "block", split_axis=1, concat_axis=0, tiled=True)
    )
    first_results = (
        combine(left_first, sectioned_first),
        combine(left_gate, sectioned_gate),
        sectioned_first,
        sectioned_gate,
    )
    value_parts = first_results[0]
    gate_parts = first_results[1]
    sectioned_first = first_results[2]
    sectioned_gate = first_results[3]
    value = value_parts.reshape(rows, count)
    gate = gate_parts.reshape(rows, count)
    sigma = jax.nn.sigmoid(gate)
    hidden = (value * gate * sigma).astype(jnp.bfloat16)
    send_mix = outgoing(right_mix, hidden, groups)
    sectioned = arrange(lax.all_to_all(send_mix, "block", split_axis=1, concat_axis=0, tiled=True))
    mixed_parts = combine(left_mix, sectioned)
    outputs = (inputs.astype(jnp.float32) + mixed_parts.reshape(rows, count)).astype(jnp.bfloat16)
    grad_rows = grad_out.reshape(left_mix.shape[0], left_mix.shape[1], count)
    grad_left_mix, back_mix = left_grads(left_mix, sectioned, grad_rows, groups)
    back_mix = lax.all_to_all(back_mix, "block", split_axis=1, concat_axis=1, tiled=True)
    back_mix = back_mix.reshape(right_mix.shape[0], right_mix.shape[1], count)
    grad_right_mix, grad_hidden = right_grads(right_mix, back_mix, hidden)
    grad_value = (grad_hidden * gate * sigma).astype(jnp.bfloat16)
    grad_gate = (grad_hidden * value * sigma * (1.0 + gate * (1.0 - sigma))).astype(jnp.bfloat16)
    value_rows = grad_value.reshape(left_first.shape[0], left_first.shape[1], count)
    gate_grad_rows = grad_gate.reshape(left_gate.shape[0], left_gate.shape[1], count)
    grad_left_first, back_first = left_grads(left_first, sectioned_first, value_rows, groups)
    grad_left_gate, back_gate = left_grads(left_gate, sectioned_gate, gate_grad_rows, groups)
    back_first, back_gate = (
        lax.all_to_all(back_first, "block", split_axis=1, concat_axis=1, tiled=True),
        lax.all_to_all(back_gate, "block", split_axis=1, concat_axis=1, tiled=True),
    )
    back_first = back_first.reshape(right_first.shape[0], right_first.shape[1], count)
    back_gate = back_gate.reshape(right_gate.shape[0], right_gate.shape[1], count)
    grad_right_first, through_first = right_grads(right_first, back_first, inputs)
    grad_right_gate, through_gate = right_grads(right_gate, back_gate, inputs)
    grad_in = (grad_out.astype(jnp.float32) + through_first + through_gate).astype(jnp.bfloat16)
    (
        summed_right_first,
        summed_left_first,
        summed_right_gate,
        summed_left_gate,
        summed_right_mix,
        summed_left_mix,
    ) = (
        lax.psum_scatter(
            grad_right_first.astype(jnp.bfloat16), "dp", scatter_dimension=1, tiled=True
        ).astype(jnp.float32),
        lax.psum_scatter(
            grad_left_first.astype(jnp.bfloat16), "dp", scatter_dimension=1, tiled=True
        ).astype(jnp.float32),
        lax.psum_scatter(
            grad_right_gate.astype(jnp.bfloat16), "dp", scatter_dimension=1, tiled=True
        ).astype(jnp.float32),
        lax.psum_scatter(
            grad_left_gate.astype(jnp.bfloat16), "dp", scatter_dimension=1, tiled=True
        ).astype(jnp.float32),
        lax.psum_scatter(
            grad_right_mix.astype(jnp.bfloat16), "dp", scatter_dimension=1, tiled=True
        ).astype(jnp.float32),
        lax.psum_scatter(
            grad_left_mix.astype(jnp.bfloat16), "dp", scatter_dimension=1, tiled=True
        ).astype(jnp.float32),
    )
    return (
        outputs,
        grad_in,
        summed_right_first,
        summed_left_first,
        summed_right_gate,
        summed_left_gate,
        summed_right_mix,
        summed_left_mix,
    )


def mm(a, b):
    return lax.dot_general(a, b, (((1,), (0,)), ((), ())), preferred_element_type=F32)


def mm_nt(a, b):
    return lax.dot_general(a, b, (((1,), (1,)), ((), ())), preferred_element_type=F32)


def fused_kernel(
    groups, nb, bs, jn, kn, chunks,
    in_ref, go_ref, rf_ref, lf_ref, rg_ref, lg_ref, rm_ref, lm_ref,
    out_ref, gin_ref, gr_ref, gl_ref,
    send_a, recv_a, send_b, recv_b, right_w, right_t, left_w, left_t, wide, gram_r, gram_l,
    right_send, right_recv, left_send, left_recv,
    send_sems, recv_sems, pair_send, pair_recv,
):
    me = lax.axis_index("block")
    dp = lax.axis_index("dp")
    other = 1 - dp
    rows, count = in_ref.shape
    tc = count // chunks
    piece = nb * jn

    barrier = pltpu.get_barrier_semaphore()

    @pl.loop(1, groups)
    def _(r):
        pl.semaphore_signal(barrier, inc=1, device_id={"block": lax.rem(me + r, groups)},
                            device_id_type=pl.DeviceIdType.MESH)

    pl.semaphore_signal(barrier, inc=1, device_id={"dp": other}, device_id_type=pl.DeviceIdType.MESH)

    def expand_right(m, ref):
        wide[...] = jnp.zeros_like(wide)
        for b in range(nb):
            wide[:, b, :, b * bs:(b + 1) * bs] = ref[b].astype(F32).reshape(groups, jn, bs)
        full = wide[...].reshape(rows, rows)
        right_w[m] = full.astype(BF16)

    def turn_right(m):
        right_t[m] = right_w[m].astype(F32).T.astype(BF16)

    spread = (
        lax.broadcasted_iota(jnp.int32, (rows, kn), 0) // jn
        == lax.broadcasted_iota(jnp.int32, (rows, kn), 1)
    ).astype(F32).astype(BF16)
    keep = (
        lax.broadcasted_iota(jnp.int32, (rows, rows), 0) // kn
        == lax.broadcasted_iota(jnp.int32, (rows, rows), 1) % jn
    )
    keep_t = (
        lax.broadcasted_iota(jnp.int32, (rows, rows), 0) % jn
        == lax.broadcasted_iota(jnp.int32, (rows, rows), 1) // kn
    )

    def expand_left(m, ref):
        left_w[m] = jnp.where(keep, mm_nt(ref[...].reshape(rows, kn), spread), 0.0).astype(BF16)

    def turn_left(m, ref):
        left_t[m] = jnp.where(keep_t, mm_nt(spread, ref[...].reshape(rows, kn)), 0.0).astype(BF16)

    def copy_to(phase, src, dst, c, r):
        peer = lax.rem(me + r, groups)
        return pltpu.make_async_remote_copy(
            src_ref=src.at[c, peer], dst_ref=dst.at[c, me],
            send_sem=send_sems.at[phase, c, r], recv_sem=recv_sems.at[phase, c, r],
            device_id={"block": peer}, device_id_type=pl.DeviceIdType.MESH,
        )

    def copy_from(phase, src, dst, c, r):
        peer = lax.rem(me + groups - r, groups)
        return pltpu.make_async_remote_copy(
            src_ref=src.at[c, peer], dst_ref=dst.at[c, peer],
            send_sem=send_sems.at[phase, c, r], recv_sem=recv_sems.at[phase, c, r],
            device_id={"block": peer}, device_id_type=pl.DeviceIdType.MESH,
        )

    def send(phase, src, dst, c):
        @pl.loop(0, groups - 1)
        def _(n):
            r = n + 1
            copy_to(phase, src, dst, c, r).start()

        dst[c, me] = src[c, me]

    def receive(phase, src, dst, c):
        @pl.loop(1, groups)
        def _(r):
            copy_from(phase, src, dst, c, r).wait_recv()

    def columns(c):
        return pl.ds(pl.multiple_of(c * tc, tc), tc)

    def put(ref, c, m, result):
        ref[c, :, m] = result.astype(BF16).reshape(groups, piece, tc)

    def take(ref, c, m):
        return ref[c, :, m].reshape(rows, tc)

    expand_right(0, rf_ref)
    expand_right(1, rg_ref)
    turn_left(2, lm_ref)

    pl.semaphore_wait(barrier, groups)

    @pl.loop(0, chunks)
    def _(c):
        v = in_ref[:, columns(c)]
        put(send_a, c, 0, mm(right_w[0], v))
        put(send_a, c, 1, mm(right_w[1], v))
        put(send_a, c, 2, mm(left_t[2], go_ref[:, columns(c)]))
        send(0, send_a, recv_a, c)

    expand_left(0, lf_ref)
    expand_left(1, lg_ref)
    expand_right(2, rm_ref)
    turn_right(2)
    turn_left(0, lf_ref)
    turn_left(1, lg_ref)
    gram_r[...] = jnp.zeros_like(gram_r)
    gram_l[...] = jnp.zeros_like(gram_l)

    @pl.loop(0, chunks)
    def _(c):
        receive(0, send_a, recv_a, c)
        first = take(recv_a, c, 0)
        gated = take(recv_a, c, 1)
        back = take(recv_a, c, 2)
        value = mm(left_w[0], first)
        gate = mm(left_w[1], gated)
        sigma = 1.0 / (1.0 + jnp.exp(-gate))
        silu = gate * sigma
        hidden = (value * silu).astype(BF16)
        put(send_b, c, 0, mm(right_w[2], hidden))
        grad_hidden = mm(right_t[2], back)
        grad_value = (grad_hidden * silu).astype(BF16)
        grad_gate = (grad_hidden * value * sigma * (1.0 + gate * (1.0 - sigma))).astype(BF16)
        put(send_b, c, 1, mm(left_t[0], grad_value))
        put(send_b, c, 2, mm(left_t[1], grad_gate))
        send(1, send_b, recv_b, c)
        gram_r[2] += mm_nt(back, hidden)
        gram_l[0] += mm_nt(grad_value, first)
        gram_l[1] += mm_nt(grad_gate, gated)

    half = bs // 2
    khalf = kn // 2

    def pick_right(m):
        full = gram_r[m].reshape(groups, nb, jn, rows)
        for b in range(nb):
            block = full[:, b, :, b * bs:(b + 1) * bs].reshape(2, half, bs)
            right_send[0, m, b] = block[0].astype(BF16)
            right_send[1, m, b] = block[1].astype(BF16)

    def pick_left(m):
        masked = jnp.where(keep, gram_l[m], 0.0).astype(BF16)
        picked = mm(masked, spread).reshape(jn, 2, khalf, kn)
        left_send[0, m] = picked[:, 0].astype(BF16)
        left_send[1, m] = picked[:, 1].astype(BF16)

    pair = {"dp": other}

    def swap(n, src, dst):
        return pltpu.make_async_remote_copy(
            src_ref=src, dst_ref=dst, send_sem=pair_send.at[n], recv_sem=pair_recv.at[n],
            device_id=pair, device_id_type=pl.DeviceIdType.MESH,
        )

    swaps = [
        swap(0, right_send.at[other, 2], right_recv.at[2]),
        swap(1, left_send.at[other, pl.ds(0, 2)], left_recv.at[pl.ds(0, 2)]),
        swap(2, right_send.at[other, pl.ds(0, 2)], right_recv.at[pl.ds(0, 2)]),
        swap(3, left_send.at[other, 2], left_recv.at[2]),
    ]
    pick_right(2)
    pick_left(0)
    pick_left(1)
    swaps[0].start()
    swaps[1].start()
    turn_right(0)
    turn_right(1)
    expand_left(2, lm_ref)

    def last_grams(c):
        receive(1, send_b, recv_b, c)
        gram_l[2] += mm_nt(go_ref[:, columns(c)], take(recv_b, c, 0))
        v = in_ref[:, columns(c)]
        gram_r[0] += mm_nt(take(recv_b, c, 1), v)
        gram_r[1] += mm_nt(take(recv_b, c, 2), v)

    def last_rows(c):
        v = in_ref[:, columns(c)]
        g = go_ref[:, columns(c)]
        out_ref[:, columns(c)] = (v.astype(F32) + mm(left_w[2], take(recv_b, c, 0))).astype(BF16)
        through = mm(right_t[0], take(recv_b, c, 1)) + mm(right_t[1], take(recv_b, c, 2))
        gin_ref[:, columns(c)] = (g.astype(F32) + through).astype(BF16)

    @pl.loop(0, chunks - 1)
    def _(c):
        last_grams(c)
        last_rows(c)

    last_grams(chunks - 1)
    pick_left(2)
    pick_right(0)
    pick_right(1)
    swaps[2].start()
    swaps[3].start()
    last_rows(chunks - 1)

    @pl.loop(0, chunks)
    def _(c):
        @pl.loop(1, groups)
        def _(r):
            copy_to(0, send_a, recv_a, c, r).wait_send()
            copy_to(1, send_b, recv_b, c, r).wait_send()

    for each in swaps:
        each.wait()
    gr_ref[...] = right_send[dp].astype(F32) + right_recv[...].astype(F32)
    gl_ref[...] = left_send[dp].astype(F32) + left_recv[...].astype(F32)


def results_kernel(
    out_in, gin_in, gr_in, gl_in, out, gin, grf, glf, grg, glg, grm, glm, rows_held, right_held, left_held, in_sems, out_sems
):
    steps = [(out_in, rows_held.at[0], out), (gin_in, rows_held.at[1], gin)]
    steps += [(gr_in.at[m], right_held.at[m], ref) for m, ref in enumerate((grf, grg, grm))]
    steps += [(gl_in.at[m], left_held.at[m], ref) for m, ref in enumerate((glf, glg, glm))]
    loads = [pltpu.make_async_copy(src, held, in_sems.at[n]) for n, (src, held, _) in enumerate(steps)]
    stores = [pltpu.make_async_copy(held, dst, out_sems.at[n]) for n, (_, held, dst) in enumerate(steps)]
    for load in loads:
        load.start()
    for load, store in zip(loads, stores):
        load.wait()
        store.start()
    for store in stores:
        store.wait()


def fused(inputs, grad_out, right_first, left_first, right_gate, left_gate, right_mix, left_mix):
    groups = lax.axis_size("block")
    rows, count = inputs.shape
    nb, bs, _ = right_first.shape
    jn, kn, _ = left_first.shape
    chunks = CHUNKS
    tc = count // chunks
    piece = nb * jn
    right_out = jax.ShapeDtypeStruct((nb, bs // 2, bs), F32)
    left_out = jax.ShapeDtypeStruct((jn, kn // 2, kn), F32)
    vmem = pl.BlockSpec(memory_space=pltpu.VMEM)
    moving = pltpu.VMEM((chunks, groups, 3, piece, tc), BF16)
    factor = pltpu.VMEM((3, rows, rows), BF16)
    moved = pl.pallas_call(
        functools.partial(fused_kernel, groups, nb, bs, jn, kn, chunks),
        out_shape=(
            jax.ShapeDtypeStruct(inputs.shape, BF16), jax.ShapeDtypeStruct(inputs.shape, BF16),
            jax.ShapeDtypeStruct((3,) + right_out.shape, F32), jax.ShapeDtypeStruct((3,) + left_out.shape, F32),
        ),
        in_specs=[vmem] * 8,
        out_specs=(vmem,) * 4,
        scratch_shapes=[
            moving, moving, moving, moving, factor, factor, factor, factor,
            pltpu.VMEM((groups, nb, jn, rows), F32),
            pltpu.VMEM((3, rows, rows), F32),
            pltpu.VMEM((3, rows, rows), F32),
            pltpu.VMEM((2, 3, nb, bs // 2, bs), BF16),
            pltpu.VMEM((3, nb, bs // 2, bs), BF16),
            pltpu.VMEM((2, 3, jn, kn // 2, kn), BF16),
            pltpu.VMEM((3, jn, kn // 2, kn), BF16),
            pltpu.SemaphoreType.DMA((2, chunks, groups)),
            pltpu.SemaphoreType.DMA((2, chunks, groups)),
            pltpu.SemaphoreType.DMA((4,)),
            pltpu.SemaphoreType.DMA((4,)),
        ],
        compiler_params=pltpu.CompilerParams(
            collective_id=0, has_side_effects=True, vmem_limit_bytes=60 * 1024 * 1024
        ),
    )(inputs, grad_out, right_first, left_first, right_gate, left_gate, right_mix, left_mix)
    anywhere = pl.BlockSpec(memory_space=pl.ANY)
    return pl.pallas_call(
        results_kernel,
        out_shape=(
            jax.ShapeDtypeStruct(inputs.shape, BF16), jax.ShapeDtypeStruct(inputs.shape, BF16),
            right_out, left_out, right_out, left_out, right_out, left_out,
        ),
        in_specs=[anywhere] * 4,
        out_specs=(anywhere,) * 8,
        scratch_shapes=[
            pltpu.VMEM((2,) + inputs.shape, BF16),
            pltpu.VMEM((3,) + right_out.shape, F32),
            pltpu.VMEM((3,) + left_out.shape, F32),
            pltpu.SemaphoreType.DMA((8,)),
            pltpu.SemaphoreType.DMA((8,)),
        ],
    )(*moved)


def layer(*args):
    groups, pairs = lax.axis_size("block"), lax.axis_size("dp")
    inputs, right, left = args[0], args[2], args[3]
    piece = right.shape[0] * left.shape[0]
    fits = (
        pairs == 2 and piece % 16 == 0 and left.shape[0] % 8 == 0 and right.shape[1] % 128 == 0
        and inputs.shape[1] % (128 * CHUNKS) == 0 and groups * piece == inputs.shape[0]
    )
    return fused(*args) if fits else shards(*args)


def solution(mesh):
    return jax.shard_map(
        layer,
        mesh=mesh,
        in_specs=(
            P("block", "dp"),
            P("block", "dp"),
            P("block", None, None),
            P("block", None, None),
            P("block", None, None),
            P("block", None, None),
            P("block", None, None),
            P("block", None, None),
        ),
        out_specs=(
            P("block", "dp"),
            P("block", "dp"),
            P("block", "dp", None),
            P("block", "dp", None),
            P("block", "dp", None),
            P("block", "dp", None),
            P("block", "dp", None),
            P("block", "dp", None),
        ),
        check_vma=False,
    )
```

```python
import functools

import jax
import jax.numpy as jnp
from jax import lax
from jax.experimental import pallas as pl
from jax.experimental.pallas import tpu as pltpu
from jax.sharding import PartitionSpec as P

F32 = jnp.float32
BF16 = jnp.bfloat16
CHUNKS = 4


def outgoing(weight, values, groups):
    shaped = values.reshape(weight.shape[0], weight.shape[2], -1)
    sectioned = jnp.einsum(
        "bik,bkt->bit", weight, shaped, preferred_element_type=jnp.float32
    ).astype(jnp.bfloat16)
    return sectioned.reshape(sectioned.shape[0], groups, -1, sectioned.shape[2])


def arrange(received):
    return received.reshape(-1, received.shape[2], received.shape[3])


def combine(weight, arranged):
    return jnp.einsum("jks,sjt->jkt", weight, arranged, preferred_element_type=jnp.float32)


def left_grads(weight, arranged, grad_rows, groups):
    grad_weight = jnp.einsum(
        "jkt,sjt->jks", grad_rows, arranged, preferred_element_type=jnp.float32
    )
    split_weight = weight.reshape(weight.shape[0], weight.shape[1], groups, -1)
    back_rows = jnp.einsum(
        "jkcr,jkt->rcjt", split_weight, grad_rows, preferred_element_type=jnp.float32
    )
    return (grad_weight, back_rows.astype(jnp.bfloat16))


def right_grads(weight, back_rows, values):
    shaped = values.reshape(weight.shape[0], weight.shape[2], -1)
    grad_weight = jnp.einsum("bit,bkt->bik", back_rows, shaped, preferred_element_type=jnp.float32)
    through = jnp.einsum("bik,bit->bkt", weight, back_rows, preferred_element_type=jnp.float32)
    return (grad_weight, through.reshape(-1, through.shape[2]))


def shards(inputs, grad_out, right_first, left_first, right_gate, left_gate, right_mix, left_mix):
    groups = lax.axis_size("block")
    rows, count = inputs.shape
    send_first = outgoing(right_first, inputs, groups)
    send_gate = outgoing(right_gate, inputs, groups)
    sectioned_first = arrange(
        lax.all_to_all(send_first, "block", split_axis=1, concat_axis=0, tiled=True)
    )
    sectioned_gate = arrange(
        lax.all_to_all(send_gate, "block", split_axis=1, concat_axis=0, tiled=True)
    )
    first_results = (
        combine(left_first, sectioned_first),
        combine(left_gate, sectioned_gate),
        sectioned_first,
        sectioned_gate,
    )
    value_parts = first_results[0]
    gate_parts = first_results[1]
    sectioned_first = first_results[2]
    sectioned_gate = first_results[3]
    value = value_parts.reshape(rows, count)
    gate = gate_parts.reshape(rows, count)
    sigma = jax.nn.sigmoid(gate)
    hidden = (value * gate * sigma).astype(jnp.bfloat16)
    send_mix = outgoing(right_mix, hidden, groups)
    sectioned = arrange(lax.all_to_all(send_mix, "block", split_axis=1, concat_axis=0, tiled=True))
    mixed_parts = combine(left_mix, sectioned)
    outputs = (inputs.astype(jnp.float32) + mixed_parts.reshape(rows, count)).astype(jnp.bfloat16)
    grad_rows = grad_out.reshape(left_mix.shape[0], left_mix.shape[1], count)
    grad_left_mix, back_mix = left_grads(left_mix, sectioned, grad_rows, groups)
    back_mix = lax.all_to_all(back_mix, "block", split_axis=1, concat_axis=1, tiled=True)
    back_mix = back_mix.reshape(right_mix.shape[0], right_mix.shape[1], count)
    grad_right_mix, grad_hidden = right_grads(right_mix, back_mix, hidden)
    grad_value = (grad_hidden * gate * sigma).astype(jnp.bfloat16)
    grad_gate = (grad_hidden * value * sigma * (1.0 + gate * (1.0 - sigma))).astype(jnp.bfloat16)
    value_rows = grad_value.reshape(left_first.shape[0], left_first.shape[1], count)
    gate_grad_rows = grad_gate.reshape(left_gate.shape[0], left_gate.shape[1], count)
    grad_left_first, back_first = left_grads(left_first, sectioned_first, value_rows, groups)
    grad_left_gate, back_gate = left_grads(left_gate, sectioned_gate, gate_grad_rows, groups)
    back_first, back_gate = (
        lax.all_to_all(back_first, "block", split_axis=1, concat_axis=1, tiled=True),
        lax.all_to_all(back_gate, "block", split_axis=1, concat_axis=1, tiled=True),
    )
    back_first = back_first.reshape(right_first.shape[0], right_first.shape[1], count)
    back_gate = back_gate.reshape(right_gate.shape[0], right_gate.shape[1], count)
    grad_right_first, through_first = right_grads(right_first, back_first, inputs)
    grad_right_gate, through_gate = right_grads(right_gate, back_gate, inputs)
    grad_in = (grad_out.astype(jnp.float32) + through_first + through_gate).astype(jnp.bfloat16)
    (
        summed_right_first,
        summed_left_first,
        summed_right_gate,
        summed_left_gate,
        summed_right_mix,
        summed_left_mix,
    ) = (
        lax.psum_scatter(
            grad_right_first.astype(jnp.bfloat16), "dp", scatter_dimension=1, tiled=True
        ).astype(jnp.float32),
        lax.psum_scatter(
            grad_left_first.astype(jnp.bfloat16), "dp", scatter_dimension=1, tiled=True
        ).astype(jnp.float32),
        lax.psum_scatter(
            grad_right_gate.astype(jnp.bfloat16), "dp", scatter_dimension=1, tiled=True
        ).astype(jnp.float32),
        lax.psum_scatter(
            grad_left_gate.astype(jnp.bfloat16), "dp", scatter_dimension=1, tiled=True
        ).astype(jnp.float32),
        lax.psum_scatter(
            grad_right_mix.astype(jnp.bfloat16), "dp", scatter_dimension=1, tiled=True
        ).astype(jnp.float32),
        lax.psum_scatter(
            grad_left_mix.astype(jnp.bfloat16), "dp", scatter_dimension=1, tiled=True
        ).astype(jnp.float32),
    )
    return (
        outputs,
        grad_in,
        summed_right_first,
        summed_left_first,
        summed_right_gate,
        summed_left_gate,
        summed_right_mix,
        summed_left_mix,
    )


def mm(a, b):
    return lax.dot_general(a, b, (((1,), (0,)), ((), ())), preferred_element_type=F32)


def mm_nt(a, b):
    return lax.dot_general(a, b, (((1,), (1,)), ((), ())), preferred_element_type=F32)


def fused_kernel(
    groups, nb, bs, jn, kn, chunks,
    in_ref, go_ref, rf_ref, lf_ref, rg_ref, lg_ref, rm_ref, lm_ref,
    out_ref, gin_ref, gr_ref, gl_ref,
    send_a, recv_a, send_b, recv_b, right_w, right_t, left_w, left_t, wide, gram_r, gram_l,
    right_send, right_recv, left_send, left_recv,
    send_sems, recv_sems, pair_send, pair_recv,
):
    me = lax.axis_index("block")
    dp = lax.axis_index("dp")
    other = 1 - dp
    rows, count = in_ref.shape
    tc = count // chunks
    piece = nb * jn

    barrier = pltpu.get_barrier_semaphore()

    @pl.loop(1, groups)
    def _(r):
        pl.semaphore_signal(barrier, inc=1, device_id={"block": lax.rem(me + r, groups)},
                            device_id_type=pl.DeviceIdType.MESH)

    pl.semaphore_signal(barrier, inc=1, device_id={"dp": other}, device_id_type=pl.DeviceIdType.MESH)

    def expand_right(m, ref):
        wide[...] = jnp.zeros_like(wide)
        for b in range(nb):
            wide[:, b, :, b * bs:(b + 1) * bs] = ref[b].astype(F32).reshape(groups, jn, bs)
        full = wide[...].reshape(rows, rows)
        right_w[m] = full.astype(BF16)

    def turn_right(m):
        right_t[m] = right_w[m].astype(F32).T.astype(BF16)

    spread = (
        lax.broadcasted_iota(jnp.int32, (rows, kn), 0) // jn
        == lax.broadcasted_iota(jnp.int32, (rows, kn), 1)
    ).astype(F32).astype(BF16)
    keep = (
        lax.broadcasted_iota(jnp.int32, (rows, rows), 0) // kn
        == lax.broadcasted_iota(jnp.int32, (rows, rows), 1) % jn
    )
    keep_t = (
        lax.broadcasted_iota(jnp.int32, (rows, rows), 0) % jn
        == lax.broadcasted_iota(jnp.int32, (rows, rows), 1) // kn
    )

    def expand_left(m, ref):
        left_w[m] = jnp.where(keep, mm_nt(ref[...].reshape(rows, kn), spread), 0.0).astype(BF16)

    def turn_left(m, ref):
        left_t[m] = jnp.where(keep_t, mm_nt(spread, ref[...].reshape(rows, kn)), 0.0).astype(BF16)

    def copy_to(phase, src, dst, c, r):
        peer = lax.rem(me + r, groups)
        return pltpu.make_async_remote_copy(
            src_ref=src.at[c, peer], dst_ref=dst.at[c, me],
            send_sem=send_sems.at[phase, c, r], recv_sem=recv_sems.at[phase, c, r],
            device_id={"block": peer}, device_id_type=pl.DeviceIdType.MESH,
        )

    def copy_from(phase, src, dst, c, r):
        peer = lax.rem(me + groups - r, groups)
        return pltpu.make_async_remote_copy(
            src_ref=src.at[c, peer], dst_ref=dst.at[c, peer],
            send_sem=send_sems.at[phase, c, r], recv_sem=recv_sems.at[phase, c, r],
            device_id={"block": peer}, device_id_type=pl.DeviceIdType.MESH,
        )

    def pair_copy(p, r, incoming):
        peer = lax.rem(me + groups - r, groups) if incoming else lax.rem(me + r, groups)
        return pltpu.make_async_remote_copy(
            src_ref=send_a.at[pl.ds(2 * p, 2), peer],
            dst_ref=recv_a.at[pl.ds(2 * p, 2), peer if incoming else me],
            send_sem=send_sems.at[0, p, r], recv_sem=recv_sems.at[0, p, r],
            device_id={"block": peer}, device_id_type=pl.DeviceIdType.MESH,
        )

    def send(phase, src, dst, c):
        @pl.loop(0, groups - 1)
        def _(n):
            r = n + 1
            copy_to(phase, src, dst, c, r).start()

        dst[c, me] = src[c, me]

    def receive(phase, src, dst, c):
        @pl.loop(1, groups)
        def _(r):
            copy_from(phase, src, dst, c, r).wait_recv()

    def columns(c):
        return pl.ds(pl.multiple_of(c * tc, tc), tc)

    def put(ref, c, m, result):
        ref[c, :, m] = result.astype(BF16).reshape(groups, piece, tc)

    def take(ref, c, m):
        return ref[c, :, m].reshape(rows, tc)

    expand_right(0, rf_ref)
    expand_right(1, rg_ref)
    turn_left(2, lm_ref)

    pl.semaphore_wait(barrier, groups)

    @pl.loop(0, chunks // 2)
    def _(p):
        for n in range(2):
            c = 2 * p + n
            v = in_ref[:, columns(c)]
            put(send_a, c, 0, mm(right_w[0], v))
            put(send_a, c, 1, mm(right_w[1], v))
            put(send_a, c, 2, mm(left_t[2], go_ref[:, columns(c)]))
            recv_a[c, me] = send_a[c, me]

        @pl.loop(1, groups)
        def _(r):
            pair_copy(p, r, False).start()

    expand_left(0, lf_ref)
    expand_left(1, lg_ref)
    expand_right(2, rm_ref)
    turn_right(2)
    turn_left(0, lf_ref)
    turn_left(1, lg_ref)
    gram_r[...] = jnp.zeros_like(gram_r)
    gram_l[...] = jnp.zeros_like(gram_l)

    @pl.loop(0, chunks)
    def _(c):
        @pl.when(lax.rem(c, 2) == 0)
        def _():
            @pl.loop(1, groups)
            def _(r):
                pair_copy(c // 2, r, True).wait_recv()

        first = take(recv_a, c, 0)
        gated = take(recv_a, c, 1)
        back = take(recv_a, c, 2)
        value = mm(left_w[0], first)
        gate = mm(left_w[1], gated)
        sigma = 1.0 / (1.0 + jnp.exp(-gate))
        silu = gate * sigma
        hidden = (value * silu).astype(BF16)
        put(send_b, c, 0, mm(right_w[2], hidden))
        grad_hidden = mm(right_t[2], back)
        grad_value = (grad_hidden * silu).astype(BF16)
        grad_gate = (grad_hidden * value * sigma * (1.0 + gate * (1.0 - sigma))).astype(BF16)
        put(send_b, c, 1, mm(left_t[0], grad_value))
        put(send_b, c, 2, mm(left_t[1], grad_gate))
        send(1, send_b, recv_b, c)
        gram_r[2] += mm_nt(back, hidden)
        gram_l[0] += mm_nt(grad_value, first)
        gram_l[1] += mm_nt(grad_gate, gated)

    half = bs // 2
    khalf = kn // 2

    def pick_right(m):
        full = gram_r[m].reshape(groups, nb, jn, rows)
        for b in range(nb):
            block = full[:, b, :, b * bs:(b + 1) * bs].reshape(2, half, bs)
            right_send[0, m, b] = block[0].astype(BF16)
            right_send[1, m, b] = block[1].astype(BF16)

    def pick_left(m):
        masked = jnp.where(keep, gram_l[m], 0.0).astype(BF16)
        picked = mm(masked, spread).reshape(jn, 2, khalf, kn)
        left_send[0, m] = picked[:, 0].astype(BF16)
        left_send[1, m] = picked[:, 1].astype(BF16)

    pair = {"dp": other}

    def swap(n, src, dst):
        return pltpu.make_async_remote_copy(
            src_ref=src, dst_ref=dst, send_sem=pair_send.at[n], recv_sem=pair_recv.at[n],
            device_id=pair, device_id_type=pl.DeviceIdType.MESH,
        )

    swaps = [
        swap(0, right_send.at[other, 2], right_recv.at[2]),
        swap(1, left_send.at[other, pl.ds(0, 2)], left_recv.at[pl.ds(0, 2)]),
        swap(2, right_send.at[other, pl.ds(0, 2)], right_recv.at[pl.ds(0, 2)]),
        swap(3, left_send.at[other, 2], left_recv.at[2]),
    ]
    pick_right(2)
    pick_left(0)
    pick_left(1)
    swaps[0].start()
    swaps[1].start()
    turn_right(0)
    turn_right(1)
    expand_left(2, lm_ref)

    def last_grams(c):
        receive(1, send_b, recv_b, c)
        gram_l[2] += mm_nt(go_ref[:, columns(c)], take(recv_b, c, 0))
        v = in_ref[:, columns(c)]
        gram_r[0] += mm_nt(take(recv_b, c, 1), v)
        gram_r[1] += mm_nt(take(recv_b, c, 2), v)

    def last_rows(c):
        v = in_ref[:, columns(c)]
        g = go_ref[:, columns(c)]
        out_ref[:, columns(c)] = (v.astype(F32) + mm(left_w[2], take(recv_b, c, 0))).astype(BF16)
        through = mm(right_t[0], take(recv_b, c, 1)) + mm(right_t[1], take(recv_b, c, 2))
        gin_ref[:, columns(c)] = (g.astype(F32) + through).astype(BF16)

    @pl.loop(0, chunks - 1)
    def _(c):
        last_grams(c)
        last_rows(c)

    last_grams(chunks - 1)
    pick_left(2)
    pick_right(0)
    pick_right(1)
    swaps[2].start()
    swaps[3].start()
    last_rows(chunks - 1)

    @pl.loop(1, groups)
    def _(r):
        @pl.loop(0, chunks // 2)
        def _(p):
            pair_copy(p, r, False).wait_send()

        @pl.loop(0, chunks)
        def _(c):
            copy_to(1, send_b, recv_b, c, r).wait_send()

    for each in swaps:
        each.wait()
    gr_ref[...] = right_send[dp].astype(F32) + right_recv[...].astype(F32)
    gl_ref[...] = left_send[dp].astype(F32) + left_recv[...].astype(F32)


def results_kernel(
    out_in, gin_in, gr_in, gl_in, out, gin, grf, glf, grg, glg, grm, glm, rows_held, right_held, left_held, in_sems, out_sems
):
    steps = [(out_in, rows_held.at[0], out), (gin_in, rows_held.at[1], gin)]
    steps += [(gr_in.at[m], right_held.at[m], ref) for m, ref in enumerate((grf, grg, grm))]
    steps += [(gl_in.at[m], left_held.at[m], ref) for m, ref in enumerate((glf, glg, glm))]
    loads = [pltpu.make_async_copy(src, held, in_sems.at[n]) for n, (src, held, _) in enumerate(steps)]
    stores = [pltpu.make_async_copy(held, dst, out_sems.at[n]) for n, (_, held, dst) in enumerate(steps)]
    for load in loads:
        load.start()
    for load, store in zip(loads, stores):
        load.wait()
        store.start()
    for store in stores:
        store.wait()


def fused(inputs, grad_out, right_first, left_first, right_gate, left_gate, right_mix, left_mix):
    groups = lax.axis_size("block")
    rows, count = inputs.shape
    nb, bs, _ = right_first.shape
    jn, kn, _ = left_first.shape
    chunks = CHUNKS
    tc = count // chunks
    piece = nb * jn
    right_out = jax.ShapeDtypeStruct((nb, bs // 2, bs), F32)
    left_out = jax.ShapeDtypeStruct((jn, kn // 2, kn), F32)
    vmem = pl.BlockSpec(memory_space=pltpu.VMEM)
    moving = pltpu.VMEM((chunks, groups, 3, piece, tc), BF16)
    factor = pltpu.VMEM((3, rows, rows), BF16)
    moved = pl.pallas_call(
        functools.partial(fused_kernel, groups, nb, bs, jn, kn, chunks),
        out_shape=(
            jax.ShapeDtypeStruct(inputs.shape, BF16), jax.ShapeDtypeStruct(inputs.shape, BF16),
            jax.ShapeDtypeStruct((3,) + right_out.shape, F32), jax.ShapeDtypeStruct((3,) + left_out.shape, F32),
        ),
        in_specs=[vmem] * 8,
        out_specs=(vmem,) * 4,
        scratch_shapes=[
            moving, moving, moving, moving, factor, factor, factor, factor,
            pltpu.VMEM((groups, nb, jn, rows), F32),
            pltpu.VMEM((3, rows, rows), F32),
            pltpu.VMEM((3, rows, rows), F32),
            pltpu.VMEM((2, 3, nb, bs // 2, bs), BF16),
            pltpu.VMEM((3, nb, bs // 2, bs), BF16),
            pltpu.VMEM((2, 3, jn, kn // 2, kn), BF16),
            pltpu.VMEM((3, jn, kn // 2, kn), BF16),
            pltpu.SemaphoreType.DMA((2, chunks, groups)),
            pltpu.SemaphoreType.DMA((2, chunks, groups)),
            pltpu.SemaphoreType.DMA((4,)),
            pltpu.SemaphoreType.DMA((4,)),
        ],
        compiler_params=pltpu.CompilerParams(
            collective_id=0, has_side_effects=True, vmem_limit_bytes=60 * 1024 * 1024
        ),
    )(inputs, grad_out, right_first, left_first, right_gate, left_gate, right_mix, left_mix)
    anywhere = pl.BlockSpec(memory_space=pl.ANY)
    return pl.pallas_call(
        results_kernel,
        out_shape=(
            jax.ShapeDtypeStruct(inputs.shape, BF16), jax.ShapeDtypeStruct(inputs.shape, BF16),
            right_out, left_out, right_out, left_out, right_out, left_out,
        ),
        in_specs=[anywhere] * 4,
        out_specs=(anywhere,) * 8,
        scratch_shapes=[
            pltpu.VMEM((2,) + inputs.shape, BF16),
            pltpu.VMEM((3,) + right_out.shape, F32),
            pltpu.VMEM((3,) + left_out.shape, F32),
            pltpu.SemaphoreType.DMA((8,)),
            pltpu.SemaphoreType.DMA((8,)),
        ],
    )(*moved)


def layer(*args):
    groups, pairs = lax.axis_size("block"), lax.axis_size("dp")
    inputs, right, left = args[0], args[2], args[3]
    piece = right.shape[0] * left.shape[0]
    fits = (
        pairs == 2 and piece % 16 == 0 and left.shape[0] % 8 == 0 and right.shape[1] % 128 == 0
        and inputs.shape[1] % (128 * CHUNKS) == 0 and groups * piece == inputs.shape[0]
    )
    return fused(*args) if fits else shards(*args)


def solution(mesh):
    return jax.shard_map(
        layer,
        mesh=mesh,
        in_specs=(
            P("block", "dp"),
            P("block", "dp"),
            P("block", None, None),
            P("block", None, None),
            P("block", None, None),
            P("block", None, None),
            P("block", None, None),
            P("block", None, None),
        ),
        out_specs=(
            P("block", "dp"),
            P("block", "dp"),
            P("block", "dp", None),
            P("block", "dp", None),
            P("block", "dp", None),
            P("block", "dp", None),
            P("block", "dp", None),
            P("block", "dp", None),
        ),
        check_vma=False,
    )
```

```python
import functools

import jax
import jax.numpy as jnp
from jax import lax
from jax.experimental import pallas as pl
from jax.experimental.pallas import tpu as pltpu
from jax.sharding import PartitionSpec as P

F32 = jnp.float32
BF16 = jnp.bfloat16
CHUNKS = 4


def outgoing(weight, values, groups):
    shaped = values.reshape(weight.shape[0], weight.shape[2], -1)
    sectioned = jnp.einsum(
        "bik,bkt->bit", weight, shaped, preferred_element_type=jnp.float32
    ).astype(jnp.bfloat16)
    return sectioned.reshape(sectioned.shape[0], groups, -1, sectioned.shape[2])


def arrange(received):
    return received.reshape(-1, received.shape[2], received.shape[3])


def combine(weight, arranged):
    return jnp.einsum("jks,sjt->jkt", weight, arranged, preferred_element_type=jnp.float32)


def left_grads(weight, arranged, grad_rows, groups):
    grad_weight = jnp.einsum(
        "jkt,sjt->jks", grad_rows, arranged, preferred_element_type=jnp.float32
    )
    split_weight = weight.reshape(weight.shape[0], weight.shape[1], groups, -1)
    back_rows = jnp.einsum(
        "jkcr,jkt->rcjt", split_weight, grad_rows, preferred_element_type=jnp.float32
    )
    return (grad_weight, back_rows.astype(jnp.bfloat16))


def right_grads(weight, back_rows, values):
    shaped = values.reshape(weight.shape[0], weight.shape[2], -1)
    grad_weight = jnp.einsum("bit,bkt->bik", back_rows, shaped, preferred_element_type=jnp.float32)
    through = jnp.einsum("bik,bit->bkt", weight, back_rows, preferred_element_type=jnp.float32)
    return (grad_weight, through.reshape(-1, through.shape[2]))


def shards(inputs, grad_out, right_first, left_first, right_gate, left_gate, right_mix, left_mix):
    groups = lax.axis_size("block")
    rows, count = inputs.shape
    send_first = outgoing(right_first, inputs, groups)
    send_gate = outgoing(right_gate, inputs, groups)
    sectioned_first = arrange(
        lax.all_to_all(send_first, "block", split_axis=1, concat_axis=0, tiled=True)
    )
    sectioned_gate = arrange(
        lax.all_to_all(send_gate, "block", split_axis=1, concat_axis=0, tiled=True)
    )
    first_results = (
        combine(left_first, sectioned_first),
        combine(left_gate, sectioned_gate),
        sectioned_first,
        sectioned_gate,
    )
    value_parts = first_results[0]
    gate_parts = first_results[1]
    sectioned_first = first_results[2]
    sectioned_gate = first_results[3]
    value = value_parts.reshape(rows, count)
    gate = gate_parts.reshape(rows, count)
    sigma = jax.nn.sigmoid(gate)
    hidden = (value * gate * sigma).astype(jnp.bfloat16)
    send_mix = outgoing(right_mix, hidden, groups)
    sectioned = arrange(lax.all_to_all(send_mix, "block", split_axis=1, concat_axis=0, tiled=True))
    mixed_parts = combine(left_mix, sectioned)
    outputs = (inputs.astype(jnp.float32) + mixed_parts.reshape(rows, count)).astype(jnp.bfloat16)
    grad_rows = grad_out.reshape(left_mix.shape[0], left_mix.shape[1], count)
    grad_left_mix, back_mix = left_grads(left_mix, sectioned, grad_rows, groups)
    back_mix = lax.all_to_all(back_mix, "block", split_axis=1, concat_axis=1, tiled=True)
    back_mix = back_mix.reshape(right_mix.shape[0], right_mix.shape[1], count)
    grad_right_mix, grad_hidden = right_grads(right_mix, back_mix, hidden)
    grad_value = (grad_hidden * gate * sigma).astype(jnp.bfloat16)
    grad_gate = (grad_hidden * value * sigma * (1.0 + gate * (1.0 - sigma))).astype(jnp.bfloat16)
    value_rows = grad_value.reshape(left_first.shape[0], left_first.shape[1], count)
    gate_grad_rows = grad_gate.reshape(left_gate.shape[0], left_gate.shape[1], count)
    grad_left_first, back_first = left_grads(left_first, sectioned_first, value_rows, groups)
    grad_left_gate, back_gate = left_grads(left_gate, sectioned_gate, gate_grad_rows, groups)
    back_first, back_gate = (
        lax.all_to_all(back_first, "block", split_axis=1, concat_axis=1, tiled=True),
        lax.all_to_all(back_gate, "block", split_axis=1, concat_axis=1, tiled=True),
    )
    back_first = back_first.reshape(right_first.shape[0], right_first.shape[1], count)
    back_gate = back_gate.reshape(right_gate.shape[0], right_gate.shape[1], count)
    grad_right_first, through_first = right_grads(right_first, back_first, inputs)
    grad_right_gate, through_gate = right_grads(right_gate, back_gate, inputs)
    grad_in = (grad_out.astype(jnp.float32) + through_first + through_gate).astype(jnp.bfloat16)
    (
        summed_right_first,
        summed_left_first,
        summed_right_gate,
        summed_left_gate,
        summed_right_mix,
        summed_left_mix,
    ) = (
        lax.psum_scatter(
            grad_right_first.astype(jnp.bfloat16), "dp", scatter_dimension=1, tiled=True
        ).astype(jnp.float32),
        lax.psum_scatter(
            grad_left_first.astype(jnp.bfloat16), "dp", scatter_dimension=1, tiled=True
        ).astype(jnp.float32),
        lax.psum_scatter(
            grad_right_gate.astype(jnp.bfloat16), "dp", scatter_dimension=1, tiled=True
        ).astype(jnp.float32),
        lax.psum_scatter(
            grad_left_gate.astype(jnp.bfloat16), "dp", scatter_dimension=1, tiled=True
        ).astype(jnp.float32),
        lax.psum_scatter(
            grad_right_mix.astype(jnp.bfloat16), "dp", scatter_dimension=1, tiled=True
        ).astype(jnp.float32),
        lax.psum_scatter(
            grad_left_mix.astype(jnp.bfloat16), "dp", scatter_dimension=1, tiled=True
        ).astype(jnp.float32),
    )
    return (
        outputs,
        grad_in,
        summed_right_first,
        summed_left_first,
        summed_right_gate,
        summed_left_gate,
        summed_right_mix,
        summed_left_mix,
    )


def mm(a, b):
    return lax.dot_general(a, b, (((1,), (0,)), ((), ())), preferred_element_type=F32)


def mm_nt(a, b):
    return lax.dot_general(a, b, (((1,), (1,)), ((), ())), preferred_element_type=F32)


def fused_kernel(
    groups, nb, bs, jn, kn, chunks,
    in_ref, go_ref, rf_ref, lf_ref, rg_ref, lg_ref, rm_ref, lm_ref,
    out_ref, gin_ref, gr_ref, gl_ref,
    send_a, recv_a, send_b, recv_b, right_w, right_t, left_w, left_t, wide, gram_r, gram_l,
    right_send, right_recv, left_send, left_recv,
    send_sems, recv_sems, pair_send, pair_recv,
):
    me = lax.axis_index("block")
    dp = lax.axis_index("dp")
    other = 1 - dp
    rows, count = in_ref.shape
    tc = count // chunks
    piece = nb * jn

    barrier = pltpu.get_barrier_semaphore()

    @pl.loop(1, groups)
    def _(r):
        pl.semaphore_signal(barrier, inc=1, device_id={"block": lax.rem(me + r, groups)},
                            device_id_type=pl.DeviceIdType.MESH)

    pl.semaphore_signal(barrier, inc=1, device_id={"dp": other}, device_id_type=pl.DeviceIdType.MESH)

    def expand_right(m, ref):
        wide[...] = jnp.zeros_like(wide)
        for b in range(nb):
            wide[:, b, :, b * bs:(b + 1) * bs] = ref[b].astype(F32).reshape(groups, jn, bs)
        full = wide[...].reshape(rows, rows)
        right_w[m] = full.astype(BF16)

    def turn_right(m):
        right_t[m] = right_w[m].astype(F32).T.astype(BF16)

    spread = (
        lax.broadcasted_iota(jnp.int32, (rows, kn), 0) // jn
        == lax.broadcasted_iota(jnp.int32, (rows, kn), 1)
    ).astype(F32).astype(BF16)
    keep = (
        lax.broadcasted_iota(jnp.int32, (rows, rows), 0) // kn
        == lax.broadcasted_iota(jnp.int32, (rows, rows), 1) % jn
    )
    keep_t = (
        lax.broadcasted_iota(jnp.int32, (rows, rows), 0) % jn
        == lax.broadcasted_iota(jnp.int32, (rows, rows), 1) // kn
    )

    def expand_left(m, ref):
        left_w[m] = jnp.where(keep, mm_nt(ref[...].reshape(rows, kn), spread), 0.0).astype(BF16)

    def turn_left(m, ref):
        left_t[m] = jnp.where(keep_t, mm_nt(spread, ref[...].reshape(rows, kn)), 0.0).astype(BF16)

    def copy_to(phase, src, dst, c, r):
        peer = lax.rem(me + r, groups)
        return pltpu.make_async_remote_copy(
            src_ref=src.at[c, peer], dst_ref=dst.at[c, me],
            send_sem=send_sems.at[phase, c, r], recv_sem=recv_sems.at[phase, c, r],
            device_id={"block": peer}, device_id_type=pl.DeviceIdType.MESH,
        )

    def copy_from(phase, src, dst, c, r):
        peer = lax.rem(me + groups - r, groups)
        return pltpu.make_async_remote_copy(
            src_ref=src.at[c, peer], dst_ref=dst.at[c, peer],
            send_sem=send_sems.at[phase, c, r], recv_sem=recv_sems.at[phase, c, r],
            device_id={"block": peer}, device_id_type=pl.DeviceIdType.MESH,
        )

    def send(phase, src, dst, c):
        @pl.loop(0, groups - 1)
        def _(n):
            r = n + 1
            copy_to(phase, src, dst, c, r).start()

        dst[c, me] = src[c, me]

    def receive(phase, src, dst, c):
        @pl.loop(1, groups)
        def _(r):
            copy_from(phase, src, dst, c, r).wait_recv()

    def columns(c):
        return pl.ds(pl.multiple_of(c * tc, tc), tc)

    def put(ref, c, m, result):
        ref[c, :, m] = result.astype(BF16).reshape(groups, piece, tc)

    def take(ref, c, m):
        return ref[c, :, m].reshape(rows, tc)

    expand_right(0, rf_ref)
    expand_right(1, rg_ref)
    turn_left(2, lm_ref)

    pl.semaphore_wait(barrier, groups)

    @pl.loop(0, chunks)
    def _(c):
        v = in_ref[:, columns(c)]
        put(send_a, c, 0, mm(right_w[0], v))
        put(send_a, c, 1, mm(right_w[1], v))
        put(send_a, c, 2, mm(left_t[2], go_ref[:, columns(c)]))
        send(0, send_a, recv_a, c)

    expand_left(0, lf_ref)
    expand_left(1, lg_ref)
    expand_right(2, rm_ref)
    turn_right(2)
    turn_left(0, lf_ref)
    turn_left(1, lg_ref)
    gram_r[...] = jnp.zeros_like(gram_r)
    gram_l[...] = jnp.zeros_like(gram_l)

    @pl.loop(0, chunks)
    def _(c):
        receive(0, send_a, recv_a, c)
        first = take(recv_a, c, 0)
        gated = take(recv_a, c, 1)
        back = take(recv_a, c, 2)
        value = mm(left_w[0], first)
        gate = mm(left_w[1], gated)
        sigma = 1.0 / (1.0 + jnp.exp(-gate))
        silu = gate * sigma
        hidden = (value * silu).astype(BF16)
        put(send_b, c, 0, mm(right_w[2], hidden))
        grad_hidden = mm(right_t[2], back)
        grad_value = (grad_hidden * silu).astype(BF16)
        grad_gate = (grad_hidden * value * sigma * (1.0 + gate * (1.0 - sigma))).astype(BF16)
        put(send_b, c, 1, mm(left_t[0], grad_value))
        put(send_b, c, 2, mm(left_t[1], grad_gate))
        send(1, send_b, recv_b, c)
        gram_r[2] += mm_nt(back, hidden)
        gram_l[0] += mm_nt(grad_value, first)
        gram_l[1] += mm_nt(grad_gate, gated)

    half = bs // 2
    khalf = kn // 2

    def pick_right(m):
        full = gram_r[m].reshape(groups, nb, jn, rows)
        for b in range(nb):
            block = full[:, b, :, b * bs:(b + 1) * bs].reshape(2, half, bs)
            right_send[0, m, b] = block[0].astype(BF16)
            right_send[1, m, b] = block[1].astype(BF16)

    def pick_left(m):
        masked = jnp.where(keep, gram_l[m], 0.0).astype(BF16)
        picked = mm(masked, spread).reshape(jn, 2, khalf, kn)
        left_send[0, m] = picked[:, 0].astype(BF16)
        left_send[1, m] = picked[:, 1].astype(BF16)

    pair = {"dp": other}

    def swap(n, src, dst):
        return pltpu.make_async_remote_copy(
            src_ref=src, dst_ref=dst, send_sem=pair_send.at[n], recv_sem=pair_recv.at[n],
            device_id=pair, device_id_type=pl.DeviceIdType.MESH,
        )

    swaps = [
        swap(0, right_send.at[other, 2], right_recv.at[2]),
        swap(1, left_send.at[other, pl.ds(0, 2)], left_recv.at[pl.ds(0, 2)]),
        swap(2, right_send.at[other, pl.ds(0, 2)], right_recv.at[pl.ds(0, 2)]),
        swap(3, left_send.at[other, 2], left_recv.at[2]),
    ]
    pick_right(2)
    pick_left(0)
    pick_left(1)
    swaps[0].start()
    swaps[1].start()
    turn_right(0)
    turn_right(1)
    expand_left(2, lm_ref)

    def last_grams(c):
        receive(1, send_b, recv_b, c)
        gram_l[2] += mm_nt(go_ref[:, columns(c)], take(recv_b, c, 0))
        v = in_ref[:, columns(c)]
        gram_r[0] += mm_nt(take(recv_b, c, 1), v)
        gram_r[1] += mm_nt(take(recv_b, c, 2), v)

    def last_rows(c):
        v = in_ref[:, columns(c)]
        g = go_ref[:, columns(c)]
        out_ref[:, columns(c)] = (v.astype(F32) + mm(left_w[2], take(recv_b, c, 0))).astype(BF16)
        through = mm(right_t[0], take(recv_b, c, 1)) + mm(right_t[1], take(recv_b, c, 2))
        gin_ref[:, columns(c)] = (g.astype(F32) + through).astype(BF16)

    @pl.loop(0, chunks - 1)
    def _(c):
        last_grams(c)
        last_rows(c)

    last_grams(chunks - 1)
    pick_left(2)
    pick_right(0)
    pick_right(1)
    swaps[2].start()
    swaps[3].start()
    last_rows(chunks - 1)

    @pl.loop(0, chunks)
    def _(c):
        @pl.loop(1, groups)
        def _(r):
            copy_to(0, send_a, recv_a, c, r).wait_send()
            copy_to(1, send_b, recv_b, c, r).wait_send()

    for each in swaps:
        each.wait()
    gr_ref[...] = right_send[dp].astype(F32) + right_recv[...].astype(F32)
    gl_ref[...] = left_send[dp].astype(F32) + left_recv[...].astype(F32)


def results_kernel(
    out_in, gin_in, gr_in, gl_in, out, gin, grf, glf, grg, glg, grm, glm, rows_held, right_held, left_held, in_sems, out_sems
):
    quarter = out.shape[0] // 4
    steps = []
    for q in range(4):
        part = pl.ds(q * quarter, quarter)
        steps.append((out_in.at[part], rows_held.at[0, part], out.at[part]))
        steps.append((gin_in.at[part], rows_held.at[1, part], gin.at[part]))
    steps += [(gr_in.at[m], right_held.at[m], ref) for m, ref in enumerate((grf, grg, grm))]
    steps += [(gl_in.at[m], left_held.at[m], ref) for m, ref in enumerate((glf, glg, glm))]
    loads = [pltpu.make_async_copy(src, held, in_sems.at[n]) for n, (src, held, _) in enumerate(steps)]
    stores = [pltpu.make_async_copy(held, dst, out_sems.at[n]) for n, (_, held, dst) in enumerate(steps)]
    for load in loads:
        load.start()
    for load, store in zip(loads, stores):
        load.wait()
        store.start()
    for store in stores:
        store.wait()


def fused(inputs, grad_out, right_first, left_first, right_gate, left_gate, right_mix, left_mix):
    groups = lax.axis_size("block")
    rows, count = inputs.shape
    nb, bs, _ = right_first.shape
    jn, kn, _ = left_first.shape
    chunks = CHUNKS
    tc = count // chunks
    piece = nb * jn
    right_out = jax.ShapeDtypeStruct((nb, bs // 2, bs), F32)
    left_out = jax.ShapeDtypeStruct((jn, kn // 2, kn), F32)
    vmem = pl.BlockSpec(memory_space=pltpu.VMEM)
    moving = pltpu.VMEM((chunks, groups, 3, piece, tc), BF16)
    factor = pltpu.VMEM((3, rows, rows), BF16)
    moved = pl.pallas_call(
        functools.partial(fused_kernel, groups, nb, bs, jn, kn, chunks),
        out_shape=(
            jax.ShapeDtypeStruct(inputs.shape, BF16), jax.ShapeDtypeStruct(inputs.shape, BF16),
            jax.ShapeDtypeStruct((3,) + right_out.shape, F32), jax.ShapeDtypeStruct((3,) + left_out.shape, F32),
        ),
        in_specs=[vmem] * 8,
        out_specs=(vmem,) * 4,
        scratch_shapes=[
            moving, moving, moving, moving, factor, factor, factor, factor,
            pltpu.VMEM((groups, nb, jn, rows), F32),
            pltpu.VMEM((3, rows, rows), F32),
            pltpu.VMEM((3, rows, rows), F32),
            pltpu.VMEM((2, 3, nb, bs // 2, bs), BF16),
            pltpu.VMEM((3, nb, bs // 2, bs), BF16),
            pltpu.VMEM((2, 3, jn, kn // 2, kn), BF16),
            pltpu.VMEM((3, jn, kn // 2, kn), BF16),
            pltpu.SemaphoreType.DMA((2, chunks, groups)),
            pltpu.SemaphoreType.DMA((2, chunks, groups)),
            pltpu.SemaphoreType.DMA((4,)),
            pltpu.SemaphoreType.DMA((4,)),
        ],
        compiler_params=pltpu.CompilerParams(
            collective_id=0, has_side_effects=True, vmem_limit_bytes=60 * 1024 * 1024
        ),
    )(inputs, grad_out, right_first, left_first, right_gate, left_gate, right_mix, left_mix)
    anywhere = pl.BlockSpec(memory_space=pl.ANY)
    return pl.pallas_call(
        results_kernel,
        out_shape=(
            jax.ShapeDtypeStruct(inputs.shape, BF16), jax.ShapeDtypeStruct(inputs.shape, BF16),
            right_out, left_out, right_out, left_out, right_out, left_out,
        ),
        in_specs=[anywhere] * 4,
        out_specs=(anywhere,) * 8,
        scratch_shapes=[
            pltpu.VMEM((2,) + inputs.shape, BF16),
            pltpu.VMEM((3,) + right_out.shape, F32),
            pltpu.VMEM((3,) + left_out.shape, F32),
            pltpu.SemaphoreType.DMA((14,)),
            pltpu.SemaphoreType.DMA((14,)),
        ],
    )(*moved)


def layer(*args):
    groups, pairs = lax.axis_size("block"), lax.axis_size("dp")
    inputs, right, left = args[0], args[2], args[3]
    piece = right.shape[0] * left.shape[0]
    fits = (
        pairs == 2 and piece % 16 == 0 and left.shape[0] % 8 == 0 and right.shape[1] % 128 == 0
        and inputs.shape[1] % (128 * CHUNKS) == 0 and groups * piece == inputs.shape[0]
    )
    return fused(*args) if fits else shards(*args)


def solution(mesh):
    return jax.shard_map(
        layer,
        mesh=mesh,
        in_specs=(
            P("block", "dp"),
            P("block", "dp"),
            P("block", None, None),
            P("block", None, None),
            P("block", None, None),
            P("block", None, None),
            P("block", None, None),
            P("block", None, None),
        ),
        out_specs=(
            P("block", "dp"),
            P("block", "dp"),
            P("block", "dp", None),
            P("block", "dp", None),
            P("block", "dp", None),
            P("block", "dp", None),
            P("block", "dp", None),
            P("block", "dp", None),
        ),
        check_vma=False,
    )
```
